32 devices in a mesh: dp: 8 (over z, x), mp: 4 (over y, core).
Axes of the slice: x: 2, y: 2, z: 4, core: 2. Of those that a mesh axis runs over, the one named last changes fastest.
Arguments:
- tokens: bfloat16 [32768, 1024], P('dp'), may hold values from -12 to 12
- out_grad: bfloat16 [32768, 1024], P('dp'), may hold values from -12 to 12
- qk_weight: float32 [2, 1024, 256], P(None, 'dp'), may hold values from -0.1875 to 0.1875
- qk_first: float32 [2, 1024, 256], P(None, 'dp'), may hold values from -0.0048828125 to 0.0048828125
- qk_second: float32 [2, 1024, 256], P(None, 'dp'), may hold values from 5.839972e-07 to 2.3359887e-06
- qk_average: float32 [2, 1024, 256], P(None, 'dp'), may hold values from -0.1875 to 0.1875
- value_weight: float32 [1024, 1024], P('dp', 'mp'), may hold values from -0.1875 to 0.1875
- value_first: float32 [1024, 1024], P('dp', 'mp'), may hold values from -0.0024414062 to 0.0024414062
- value_second: float32 [1024, 1024], P('dp', 'mp'), may hold values from 1.9069296e-07 to 7.6277183e-07
- value_average: float32 [1024, 1024], P('dp', 'mp'), may hold values from -0.1875 to 0.1875
- output_weight: float32 [1024, 1024], P('mp', 'dp'), may hold values from -1.5 to 1.5
- output_first: float32 [1024, 1024], P('mp', 'dp'), may hold values from -0.00048828125 to 0.00048828125
- output_second: float32 [1024, 1024], P('mp', 'dp'), may hold values from 6.7040493e-09 to 2.6816197e-08
- output_average: float32 [1024, 1024], P('mp', 'dp'), may hold values from -1.5 to 1.5
- gate_up_weight: float32 [2, 1024, 2752], P(None, 'dp', 'mp'), may hold values from -0.1875 to 0.1875
- gate_up_first: float32 [2, 1024, 2752], P(None, 'dp', 'mp'), may hold values from -0.0009765625 to 0.0009765625
- gate_up_second: float32 [2, 1024, 2752], P(None, 'dp', 'mp'), may hold values from 3.2775354e-08 to 1.3110142e-07
- gate_up_average: float32 [2, 1024, 2752], P(None, 'dp', 'mp'), may hold values from -0.1875 to 0.1875
- down_weight: float32 [2752, 1024], P('mp', 'dp'), may hold values from -0.109375 to 0.109375
- down_first: float32 [2752, 1024], P('mp', 'dp'), may hold values from -0.001953125 to 0.001953125
- down_second: float32 [2752, 1024], P('mp', 'dp'), may hold values from 1.0726479e-07 to 4.2905916e-07
- down_average: float32 [2752, 1024], P('mp', 'dp'), may hold values from -0.109375 to 0.109375
- gains: float32 [2, 1024], P(None, 'dp'), may hold values from 0.5 to 1.5
- gains_first: float32 [2, 1024], P(None, 'dp'), may hold values from -0.0034179688 to 0.0034179688
- gains_second: float32 [2, 1024], P(None, 'dp'), may hold values from 2.9795777e-07 to 1.1918311e-06
- gains_average: float32 [2, 1024], P(None, 'dp'), may hold values from 0.5 to 1.5
Outputs:
- block_out: bfloat16 [32768, 1024], P('dp', 'mp')
- input_grad: float32 [32768, 1024], P('dp', 'mp')
- grad_norm: float32 [], replicated
- qk_first_new: float32 [2, 1024, 256], P(None, 'dp')
- qk_second_new: float32 [2, 1024, 256], P(None, 'dp')
- qk_new: float32 [2, 1024, 256], P(None, 'dp')
- qk_average_new: float32 [2, 1024, 256], P(None, 'dp')
- value_first_new: float32 [1024, 1024], P('dp', 'mp')
- value_second_new: float32 [1024, 1024], P('dp', 'mp')
- value_new: float32 [1024, 1024], P('dp', 'mp')
- value_average_new: float32 [1024, 1024], P('dp', 'mp')
- output_first_new: float32 [1024, 1024], P('mp', 'dp')
- output_second_new: float32 [1024, 1024], P('mp', 'dp')
- output_new: float32 [1024, 1024], P('mp', 'dp')
- output_average_new: float32 [1024, 1024], P('mp', 'dp')
- gate_up_first_new: float32 [2, 1024, 2752], P(None, 'dp', 'mp')
- gate_up_second_new: float32 [2, 1024, 2752], P(None, 'dp', 'mp')
- gate_up_new: float32 [2, 1024, 2752], P(None, 'dp', 'mp')
- gate_up_average_new: float32 [2, 1024, 2752], P(None, 'dp', 'mp')
- down_first_new: float32 [2752, 1024], P('mp', 'dp')
- down_second_new: float32 [2752, 1024], P('mp', 'dp')
- down_new: float32 [2752, 1024], P('mp', 'dp')
- down_average_new: float32 [2752, 1024], P('mp', 'dp')
- gains_first_new: float32 [2, 1024], P(None, 'dp')
- gains_second_new: float32 [2, 1024], P(None, 'dp')
- gains_new: float32 [2, 1024], P(None, 'dp')
- gains_average_new: float32 [2, 1024], P(None, 'dp')
The draws below stay inside these ranges and needn't reach their ends.
All inputs are finite; a program needn't handle non-finite values.
Results may differ from the reference program's by a relative error of at most 0.018.
Values may be sent and summed in bfloat16 or wider, within the bound.
A program may use at most 256 MiB of HBM per device.

```python
import math
import jax
import jax.numpy as jnp
from jax import lax

D = 1024
H = 16
F = 16
VH = 64
FF = 2752
QK = 256
V_ALL = 1024
LEN = 1024
TOK_DEV = 4096
TOKENS = 32768
STEP = 5
N_DP = 8
N_MP = 4


def feature_rise(key):
    column = jnp.arange(D).astype(jnp.float32) / max(D - 1, 1)
    factor = 3.0
    base = jnp.clip(jax.random.normal(key, (TOKENS, D), jnp.float32), -6.0, 6.0)
    scale = jnp.exp((column - 0.5) * jnp.log(factor))
    return base * scale[None, :]


def draw_tokens(key, part):
    return feature_rise(jax.random.fold_in(key, 11)).astype(jnp.bfloat16)


def draw_out_grad(key, part):
    return feature_rise(jax.random.fold_in(key, 23)).astype(jnp.bfloat16)


def levels(own_key, shape, cuts, smallest, high):
    factor_of = 1.0
    for dim, blocks in cuts:
        heights = jax.random.uniform(jax.random.fold_in(jax.random.fold_in(own_key, 6), dim), (blocks,), jnp.float32, smallest / len(cuts), high / len(cuts))
        factor_of = factor_of * jnp.repeat(jnp.exp(heights), shape[dim] // blocks).reshape((-1,) + (1,) * (len(shape) - 1 - dim))
    return factor_of


def normal_values(key, extent, width, limit, cuts=(), kind=jnp.bfloat16):
    array = width * jax.random.normal(key, extent, jnp.float32)
    if cuts:
        array = array * levels(key, extent, cuts, -0.22, 0.18)
    return jnp.clip(array, -limit, limit).astype(kind)


def setup_inputs(seed: int = 0) -> dict:
    key_of = jax.random.split(jax.random.key(seed), 27)
    tokens = draw_tokens(jax.random.fold_in(key_of[26], 71), 0)
    out_grad = draw_out_grad(jax.random.fold_in(key_of[26], 71), 0)
    qk_weight = normal_values(key_of[2], (2, D, QK), D ** -0.5, 0.1875, ((1, 8),), jnp.float32)
    qk_first = normal_values(key_of[3], (2, D, QK), (14 / (392 * D * QK + 66 * D * V_ALL + 58 * D * FF + 200 * D) ** 0.5), 0.0048828125, ((1, 8),), jnp.float32)
    qk_second = jnp.clip(jnp.exp(math.log(2.3359887109108968e-06) - 1.3862944 * jax.random.uniform(key_of[4], (2, D, QK), jnp.float32) ** levels(key_of[4], (2, D, QK), ((1, 8),), -0.2, 0.2)), 5.839971777277242e-07, 2.3359887109108968e-06)
    qk_average = normal_values(key_of[5], (2, D, QK), D ** -0.5, 0.1875, ((1, 8),), jnp.float32)
    value_weight = normal_values(key_of[6], (D, V_ALL), D ** -0.5, 0.1875, ((0, 8), (1, 4)), jnp.float32)
    value_first = normal_values(key_of[7], (D, V_ALL), (8 / (392 * D * QK + 66 * D * V_ALL + 58 * D * FF + 200 * D) ** 0.5), 0.0024414062, ((0, 8), (1, 4)), jnp.float32)
    value_second = jnp.clip(jnp.exp(math.log(7.627718332514632e-07) - 1.3862944 * jax.random.uniform(key_of[8], (D, V_ALL), jnp.float32) ** levels(key_of[8], (D, V_ALL), ((0, 8), (1, 4)), -0.2, 0.2)), 1.906929583128658e-07, 7.627718332514632e-07)
    value_average = normal_values(key_of[9], (D, V_ALL), D ** -0.5, 0.1875, ((0, 8), (1, 4)), jnp.float32)
    output_weight = normal_values(key_of[10], (V_ALL, D), (max(1, V_ALL * 16 // LEN)) ** -0.5, 1.5, ((0, 4), (1, 8)), jnp.float32)
    output_first = normal_values(key_of[11], (V_ALL, D), (1.5 / (392 * D * QK + 66 * D * V_ALL + 58 * D * FF + 200 * D) ** 0.5), 0.00048828125, ((0, 4), (1, 8)), jnp.float32)
    output_second = jnp.clip(jnp.exp(math.log(2.6816197262746755e-08) - 1.3862944 * jax.random.uniform(key_of[12], (V_ALL, D), jnp.float32) ** levels(key_of[12], (V_ALL, D), ((0, 4), (1, 8)), -0.2, 0.2)), 6.704049315686689e-09, 2.6816197262746755e-08)
    output_average = normal_values(key_of[13], (V_ALL, D), (max(1, V_ALL * 16 // LEN)) ** -0.5, 1.5, ((0, 4), (1, 8)), jnp.float32)
    gate_up_weight = normal_values(key_of[14], (2, D, FF), D ** -0.5, 0.1875, ((1, 8), (2, 4)), jnp.float32)
    gate_up_first = normal_values(key_of[15], (2, D, FF), (3.3 / (392 * D * QK + 66 * D * V_ALL + 58 * D * FF + 200 * D) ** 0.5), 0.0009765625, ((1, 8), (2, 4)), jnp.float32)
    gate_up_second = jnp.clip(jnp.exp(math.log(1.311014159455226e-07) - 1.3862944 * jax.random.uniform(key_of[16], (2, D, FF), jnp.float32) ** levels(key_of[16], (2, D, FF), ((1, 8), (2, 4)), -0.2, 0.2)), 3.277535398638065e-08, 1.311014159455226e-07)
    gate_up_average = normal_values(key_of[17], (2, D, FF), D ** -0.5, 0.1875, ((1, 8), (2, 4)), jnp.float32)
    down_weight = normal_values(key_of[18], (FF, D), FF ** -0.5, 0.109375, ((0, 4), (1, 8)), jnp.float32)
    down_first = normal_values(key_of[19], (FF, D), (6 / (392 * D * QK + 66 * D * V_ALL + 58 * D * FF + 200 * D) ** 0.5), 0.001953125, ((0, 4), (1, 8)), jnp.float32)
    down_second = jnp.clip(jnp.exp(math.log(4.290591562039481e-07) - 1.3862944 * jax.random.uniform(key_of[20], (FF, D), jnp.float32) ** levels(key_of[20], (FF, D), ((0, 4), (1, 8)), -0.2, 0.2)), 1.0726478905098702e-07, 4.290591562039481e-07)
    down_average = normal_values(key_of[21], (FF, D), FF ** -0.5, 0.109375, ((0, 4), (1, 8)), jnp.float32)
    gains = jnp.clip(1.0 + 0.1 * jax.random.normal(key_of[22], (2, D), jnp.float32), 0.5, 1.5)
    gains_first = normal_values(key_of[23], (2, D), (10 / (392 * D * QK + 66 * D * V_ALL + 58 * D * FF + 200 * D) ** 0.5), 0.0034179688, ((1, 8),), jnp.float32)
    gains_second = jnp.clip(jnp.exp(math.log(1.1918310747205396e-06) - 1.3862944 * jax.random.uniform(key_of[24], (2, D), jnp.float32) ** levels(key_of[24], (2, D), ((1, 8),), -0.2, 0.2)), 2.979577686801349e-07, 1.1918310747205396e-06)
    gains_average = jnp.clip(1.0 + 0.1 * jax.random.normal(key_of[25], (2, D), jnp.float32), 0.5, 1.5)
    return dict(tokens=tokens, out_grad=out_grad, qk_weight=qk_weight, qk_first=qk_first, qk_second=qk_second, qk_average=qk_average, value_weight=value_weight, value_first=value_first, value_second=value_second, value_average=value_average, output_weight=output_weight, output_first=output_first, output_second=output_second, output_average=output_average, gate_up_weight=gate_up_weight, gate_up_first=gate_up_first, gate_up_second=gate_up_second, gate_up_average=gate_up_average, down_weight=down_weight, down_first=down_first, down_second=down_second, down_average=down_average, gains=gains, gains_first=gains_first, gains_second=gains_second, gains_average=gains_average)


@jax.custom_vjp
def low(v):
    return lax.optimization_barrier(v.astype(jnp.bfloat16)).astype(jnp.float32)

@jax.custom_vjp
def low_back(v):
    return v

def low_keep(v):
    return (low(v), None)

def low_pass(kept, grad):
    return (grad,)

def back_keep(v):
    return (v, None)

def back_low(kept, grad):
    return (low(grad),)
low.defvjp(low_keep, low_pass)
low_back.defvjp(back_keep, back_low)

def both_ways(values):
    return low(low_back(values))

def rms_scale(values):
    return lax.rsqrt(lax.optimization_barrier(jnp.mean(values * values, axis=-1, keepdims=True)) + 1e-05)

def mix_parts(parts):
    query, keys, values = parts
    length = query.shape[0]
    causal = (jnp.arange(length)[:, None] >= jnp.arange(length)[None, :]).astype(jnp.float32)
    tiled = low_back(jnp.einsum('ihf,jhf->hij', query, keys, precision=lax.Precision.HIGHEST) / math.sqrt(F))
    kernel = causal * (1.0 + tiled + 0.5 * tiled * tiled)
    numer = low_back(jnp.einsum('hij,jhv->ihv', low(kernel), values, precision=lax.Precision.HIGHEST))
    denom = lax.optimization_barrier(jnp.sum(kernel, axis=2)).T[:, :, None]
    return numer / denom

def to_heads(grouped, size):
    count = grouped.shape[1]
    return grouped.reshape(grouped.shape[0], count, -1, size).transpose(1, 0, 2, 3).reshape(count, -1, size)

def forward(inputs, qk_weight, value_weight, output_weight, gate_up_weight, down_weight, gains):
    highest = lax.Precision.HIGHEST
    groups = N_MP
    per_group = H // groups
    tok_count = inputs.shape[0]
    seq_count = tok_count // LEN
    qk_low = low(qk_weight)
    value_low = low(value_weight)
    output_low = low(output_weight)
    gate_up_low = low(gate_up_weight)
    down_low = low(down_weight)
    gain_low = low(gains)
    copies = low_back(jnp.broadcast_to(inputs[None], (groups, tok_count, D)))
    hidden_one = low(copies * rms_scale(copies) * gain_low[0])
    query = both_ways(jnp.einsum('gtd,dgc->gtc', hidden_one, qk_low[0].reshape(D, groups, per_group * F), precision=highest))
    keys = both_ways(jnp.einsum('gtd,dgc->gtc', hidden_one, qk_low[1].reshape(D, groups, per_group * F), precision=highest))
    values = both_ways(jnp.einsum('gtd,dgc->gtc', hidden_one, value_low.reshape(D, groups, per_group * VH), precision=highest))
    query = to_heads(query, F).reshape(seq_count, LEN, H, F)
    keys = to_heads(keys, F).reshape(seq_count, LEN, H, F)
    values = to_heads(values, VH).reshape(seq_count, LEN, H, VH)
    mixed = lax.map(jax.checkpoint(mix_parts), (query, keys, values))
    mixed = low(mixed.reshape(tok_count, groups, per_group * VH).transpose(1, 0, 2))
    attn_parts = low(low_back(jnp.einsum('gtc,gcd->gtd', mixed, output_low.reshape(groups, per_group * VH, D), precision=highest)))
    resid = inputs + lax.optimization_barrier(jnp.sum(attn_parts, axis=0))
    hidden_two = low(resid * rms_scale(resid) * gain_low[1])
    twins = low_back(jnp.broadcast_to(hidden_two[None], (groups, tok_count, D)))
    gate = low_back(jnp.einsum('gtd,dgf->gtf', twins, gate_up_low[0].reshape(D, groups, FF // groups), precision=highest))
    lift = low_back(jnp.einsum('gtd,dgf->gtf', twins, gate_up_low[1].reshape(D, groups, FF // groups), precision=highest))
    activ = low(jax.nn.silu(gate) * lift)
    down_parts = low(jnp.einsum('gtf,gfd->gtd', activ, down_low.reshape(groups, FF // groups, D), precision=highest))
    return low(resid + lax.optimization_barrier(jnp.sum(down_parts, axis=0)))

def adam_step(grad, first, second, weight, average, rate):
    first = 0.5 * first + 0.5 * grad
    second = 0.5 * second + 0.5 * grad * grad
    correct = 1.0 - 0.5 ** STEP
    weight = weight - rate * (first / correct / (jnp.sqrt(second / correct) + 1e-08) + 0.1 * weight)
    average = 0.5 * average + 0.5 * weight
    return (first, second, weight, average)

def reference(tokens, out_grad, qk_weight, qk_first, qk_second, qk_average, value_weight, value_first, value_second, value_average, output_weight, output_first, output_second, output_average, gate_up_weight, gate_up_first, gate_up_second, gate_up_average, down_weight, down_first, down_second, down_average, gains, gains_first, gains_second, gains_average):
    params = (qk_weight, value_weight, output_weight, gate_up_weight, down_weight, gains)
    tok_blocks = tokens.astype(jnp.float32).reshape(N_DP, TOK_DEV, D)
    cot_blocks = out_grad.astype(jnp.float32).reshape(N_DP, TOK_DEV, D)

    def one_block(totals, pair):
        block_in, block_cot = pair
        result, pull = jax.vjp(forward, block_in, *params)
        grads = pull(block_cot)
        totals = tuple((a + b for a, b in zip(totals, grads[1:])))
        return (totals, (result.astype(jnp.bfloat16), grads[0]))
    zeros = tuple((jnp.zeros_like(p) for p in params))
    totals, (outs, input_grads) = lax.scan(one_block, zeros, (tok_blocks, cot_blocks))
    squares = jnp.float32(0.0)
    for grad in totals:
        squares = squares + jnp.sum(grad * grad)
    grad_norm = jnp.sqrt(squares)
    clip = jnp.minimum(1.0, 1.0 / (grad_norm + 1e-06))
    qk_grad, value_grad, output_grad, gate_up_grad, down_grad, gains_grad = totals
    qk_m, qk_v, qk_w, qk_a = adam_step(clip * qk_grad, qk_first, qk_second, qk_weight, qk_average, 1.0 / math.sqrt(D))
    value_m, value_v, value_w, value_a = adam_step(clip * value_grad, value_first, value_second, value_weight, value_average, 1.0 / math.sqrt(D))
    output_m, output_v, output_w, output_a = adam_step(clip * output_grad, output_first, output_second, output_weight, output_average, 1.0 / math.sqrt(max(1, V_ALL * 16 // LEN)))
    gate_up_m, gate_up_v, gate_up_w, gate_up_a = adam_step(clip * gate_up_grad, gate_up_first, gate_up_second, gate_up_weight, gate_up_average, 1.0 / math.sqrt(D))
    down_m, down_v, down_w, down_a = adam_step(clip * down_grad, down_first, down_second, down_weight, down_average, 1.0 / math.sqrt(FF))
    gains_m, gains_v, gains_w, gains_a = adam_step(clip * gains_grad, gains_first, gains_second, gains, gains_average, 0.4)
    block_out = outs.reshape(TOKENS, D)
    input_grad = input_grads.reshape(TOKENS, D)
    return (block_out, input_grad, grad_norm, qk_m, qk_v, qk_w, qk_a, value_m, value_v, value_w, value_a, output_m, output_v, output_w, output_a, gate_up_m, gate_up_v, gate_up_w, gate_up_a, down_m, down_v, down_w, down_a, gains_m, gains_v, gains_w, gains_a)
```

```python
import functools
import math

import jax
import jax.numpy as jnp
from jax import lax
from jax.experimental import pallas as pl
from jax.experimental.pallas import tpu as pltpu
from jax.sharding import PartitionSpec as P

D = 1024
H = 16
F = 16
VH = 64
FF = 2752
V_ALL = 1024
LEN = 1024
STEP = 5
BLOCK = 256


def nn(left, right):
    return lax.dot_general(
        left, right, (((1,), (0,)), ((), ())), preferred_element_type=jnp.float32
    )


def nt(left, right):
    return lax.dot_general(
        left, right, (((1,), (1,)), ((), ())), preferred_element_type=jnp.float32
    )


def tn(left, right):
    return lax.dot_general(
        left, right, (((0,), (0,)), ((), ())), preferred_element_type=jnp.float32
    )


def rms_scale(values):
    return lax.rsqrt(jnp.mean(values * values, axis=1, keepdims=True) + 1e-05)


def upper(size):
    rows = lax.broadcasted_iota(jnp.int32, (size, size), 0)
    return rows <= lax.broadcasted_iota(jnp.int32, (size, size), 1)


def spans(block):
    start = block * BLOCK
    whole = [(0, start, False)] if block else []
    return whole + [(start, start + BLOCK, True)]


def mix_forward(query_ref, keys_ref, values_ref, mixed_ref, denom_ref):
    keys = keys_ref[...].T
    seen = upper(BLOCK)
    for block in range(query_ref.shape[1] // BLOCK):
        at = slice(block * BLOCK, (block + 1) * BLOCK)
        query = query_ref[:, at] * jnp.bfloat16(1.0 / math.sqrt(F))
        numer, denom = 0.0, 0.0
        for low, high, edge in spans(block):
            slope = nn(keys[low:high], query) + 1.0
            kernel = slope * slope + 1.0
            if edge:
                kernel = jnp.where(seen, kernel, 0.0)
            denom += jnp.sum(kernel, axis=0, keepdims=True)
            numer += nn(values_ref[:, low:high], kernel.astype(jnp.bfloat16))
        mixed_ref[:, at] = (numer / denom).astype(jnp.bfloat16)
        denom_ref[0, :, at] = denom


def mix_backward(
    query_ref,
    keys_ref,
    values_ref,
    mixed_ref,
    denom_ref,
    grad_ref,
    grad_query_ref,
    grad_keys_ref,
    grad_values_ref,
    keys_sum,
    values_sum,
):
    root = 1.0 / math.sqrt(F)
    keys = keys_ref[...].T
    values = values_ref[...].T
    seen = upper(BLOCK)
    keys_sum[...] = jnp.zeros_like(keys_sum)
    values_sum[...] = jnp.zeros_like(values_sum)
    for block in range(query_ref.shape[1] // BLOCK):
        at = slice(block * BLOCK, (block + 1) * BLOCK)
        query = query_ref[:, at] * jnp.bfloat16(root)
        share = 2.0 / denom_ref[0, :, at]
        grad = grad_ref[:, at].astype(jnp.float32)
        grad_numer = (grad * share).astype(jnp.bfloat16)
        grad_denom = -share * jnp.sum(
            grad * mixed_ref[:, at].astype(jnp.float32), axis=0, keepdims=True
        )
        grad_query = 0.0
        for low, high, edge in spans(block):
            slope = nn(keys[low:high], query) + 1.0
            kernel = slope * slope + 1.0
            grad_tiled = (nn(values[low:high], grad_numer) + grad_denom) * slope
            if edge:
                kernel = jnp.where(seen, kernel, 0.0)
                grad_tiled = jnp.where(seen, grad_tiled, 0.0)
            kernel = kernel.astype(jnp.bfloat16)
            grad_tiled = grad_tiled.astype(jnp.bfloat16)
            values_sum[:, low:high] += nt(grad_numer, kernel)
            keys_sum[:, low:high] += nt(query, grad_tiled)
            grad_query += nn(keys_ref[:, low:high], grad_tiled)
        grad_query_ref[:, at] = (grad_query * root).astype(jnp.bfloat16)
    grad_keys_ref[...] = keys_sum[...].astype(jnp.bfloat16)
    grad_values_ref[...] = (values_sum[...] * 0.5).astype(jnp.bfloat16)


def head_specs(groups, count):
    here = H // groups
    small = here * (2 * F + VH) // F
    large = here * (2 * F + VH) // VH
    skip = 2 * here * F // VH
    query = pl.BlockSpec((F, count), lambda h: (h // here * small + h % here, 0))
    keys = pl.BlockSpec((F, count), lambda h: (h // here * small + here + h % here, 0))
    values = pl.BlockSpec((VH, count), lambda h: (h // here * large + skip + h % here, 0))
    return [query, keys, values]


def attend(projected, groups):
    count = projected.shape[1]
    return pl.pallas_call(
        mix_forward,
        grid=(H,),
        in_specs=head_specs(groups, count),
        out_specs=[
            pl.BlockSpec((VH, count), lambda h: (h, 0)),
            pl.BlockSpec((1, 1, count), lambda h: (h, 0, 0)),
        ],
        out_shape=[
            jax.ShapeDtypeStruct((H * VH, count), jnp.bfloat16),
            jax.ShapeDtypeStruct((H, 1, count), jnp.float32),
        ],
        cost_estimate=pl.CostEstimate(
            flops=20_000_000_000, bytes_accessed=8_000_000, transcendentals=0
        ),
        compiler_params=pltpu.CompilerParams(vmem_limit_bytes=48 << 20),
        name="attend",
    )(projected, projected, projected)


def attend_back(projected, mixed, denom, grad, groups):
    count = projected.shape[1]
    head = pl.BlockSpec((VH, count), lambda h: (h, 0))
    return pl.pallas_call(
        mix_backward,
        grid=(H,),
        in_specs=head_specs(groups, count)
        + [head, pl.BlockSpec((1, 1, count), lambda h: (h, 0, 0)), head],
        out_specs=[
            pl.BlockSpec((F, count), lambda h: (h, 0)),
            pl.BlockSpec((F, count), lambda h: (h, 0)),
            head,
        ],
        out_shape=[
            jax.ShapeDtypeStruct((H * F, count), jnp.bfloat16),
            jax.ShapeDtypeStruct((H * F, count), jnp.bfloat16),
            jax.ShapeDtypeStruct((H * VH, count), jnp.bfloat16),
        ],
        scratch_shapes=[
            pltpu.VMEM((F, count), jnp.float32),
            pltpu.VMEM((VH, count), jnp.float32),
        ],
        cost_estimate=pl.CostEstimate(
            flops=40_000_000_000, bytes_accessed=12_000_000, transcendentals=0
        ),
        compiler_params=pltpu.CompilerParams(vmem_limit_bytes=48 << 20),
        name="attend_back",
    )(projected, projected, projected, mixed, denom, grad)


def adam_step(grad, first, second, weight, average, rate):
    first = 0.5 * first + 0.5 * grad
    second = 0.5 * second + 0.5 * grad * grad
    correct = 1.0 - 0.5**STEP
    weight = weight - rate * (first / correct / (jnp.sqrt(second / correct) + 1e-08) + 0.1 * weight)
    average = 0.5 * average + 0.5 * weight
    return (first, second, weight, average)


def gather(shard):
    return lax.all_gather(
        lax.all_gather(shard, "dp", axis=1, tiled=True), "mp", axis=0, tiled=True
    )


def scatter(grad):
    return lax.psum_scatter(
        lax.psum_scatter(grad, "mp", scatter_dimension=0, tiled=True),
        "dp",
        scatter_dimension=1,
        tiled=True,
    )


def on_device(
    tokens,
    out_grad,
    qk_weight,
    qk_first,
    qk_second,
    qk_average,
    value_weight,
    value_first,
    value_second,
    value_average,
    output_weight,
    output_first,
    output_second,
    output_average,
    gate_up_weight,
    gate_up_first,
    gate_up_second,
    gate_up_average,
    down_weight,
    down_first,
    down_second,
    down_average,
    gains,
    gains_first,
    gains_second,
    gains_average,
):
    groups = lax.axis_size("mp")
    rank = lax.axis_index("mp")
    low = jnp.bfloat16
    here = H // groups
    count = tokens.shape[0] // groups
    assert count == LEN
    width = here * F
    qk_here = lax.dynamic_slice_in_dim(qk_weight, rank * width, width, 2).astype(low)
    shard_in = jnp.concatenate((qk_here[0].T, qk_here[1].T, value_weight.astype(low).T), axis=0)
    w_in = gather(shard_in)
    w_out = gather(output_weight.astype(low))
    w_gate = gather(gate_up_weight[0].astype(low).T)
    w_up = gather(gate_up_weight[1].astype(low).T)
    w_down = gather(down_weight.astype(low))
    gains_full = lax.all_gather(gains.astype(low), "dp", axis=1, tiled=True).astype(jnp.float32)
    first_gain, second_gain = gains_full[0], gains_full[1]

    inputs = lax.dynamic_slice_in_dim(tokens, rank * count, count, 0).astype(jnp.float32)
    cotan_low = lax.dynamic_slice_in_dim(out_grad, rank * count, count, 0)
    cotan = cotan_low.astype(jnp.float32)
    scale_one = rms_scale(inputs)
    hidden_one = (inputs * scale_one * first_gain).astype(low)
    projected = nt(w_in, hidden_one).astype(low)
    mixed, denom = attend(projected, groups)
    resid = inputs + tn(mixed, w_out)
    scale_two = rms_scale(resid)
    hidden_two = (resid * scale_two * second_gain).astype(low)
    gate = nt(w_gate, hidden_two)
    lift = nt(w_up, hidden_two)
    sigma = jax.nn.sigmoid(gate)
    grad_activ = nt(w_down, cotan_low)
    activ = (gate * sigma * lift).astype(low)
    grad_gate = (grad_activ * lift * sigma * (1.0 + gate * (1.0 - sigma))).astype(low)
    grad_lift = (grad_activ * gate * sigma).astype(low)
    down_grad = nn(activ, cotan_low).astype(low)
    gate_grad = nn(grad_gate, hidden_two).astype(low)
    up_grad = nn(grad_lift, hidden_two).astype(low)
    block_out = (resid + tn(activ, w_down)).astype(low)
    back_two = tn(grad_gate, w_gate) + tn(grad_lift, w_up)
    gain_two = jnp.sum(back_two * resid * scale_two, axis=0)
    grad_resid = (
        cotan
        + scale_two * second_gain * back_two
        - resid * scale_two**3 * jnp.mean(resid * second_gain * back_two, axis=1, keepdims=True)
    )
    resid_low = grad_resid.astype(low)
    output_grad = nn(mixed, resid_low).astype(low)
    grad_mixed = nt(w_out, resid_low).astype(low)
    grad_query, grad_keys, grad_values = attend_back(projected, mixed, denom, grad_mixed, groups)
    pieces = []
    for group in range(groups):
        pieces += [
            grad_query[group * width : (group + 1) * width],
            grad_keys[group * width : (group + 1) * width],
            grad_values[group * here * VH : (group + 1) * here * VH],
        ]
    grad_projected = jnp.concatenate(pieces, axis=0)
    in_grad = nn(grad_projected, hidden_one).astype(low)
    back_one = tn(grad_projected, w_in)
    gain_one = jnp.sum(back_one * inputs * scale_one, axis=0)
    input_grad = (
        grad_resid
        + scale_one * first_gain * back_one
        - inputs * scale_one**3 * jnp.mean(inputs * first_gain * back_one, axis=1, keepdims=True)
    ).astype(low)

    block_out = lax.all_to_all(block_out, "mp", split_axis=1, concat_axis=0, tiled=True)
    input_grad = lax.all_to_all(input_grad, "mp", split_axis=1, concat_axis=0, tiled=True).astype(
        jnp.float32
    )
    down_share = scatter(down_grad).astype(jnp.float32)
    gate_share = scatter(gate_grad).astype(jnp.float32)
    up_share = scatter(up_grad).astype(jnp.float32)
    output_share = scatter(output_grad).astype(jnp.float32)
    in_share = scatter(in_grad).astype(jnp.float32)
    gains_grad = lax.psum(jnp.stack((gain_one, gain_two)), "mp")
    gains_share = lax.psum_scatter(gains_grad, "dp", scatter_dimension=1, tiled=True)

    total = lax.psum(
        jnp.sum(down_share * down_share)
        + jnp.sum(gate_share * gate_share)
        + jnp.sum(up_share * up_share)
        + jnp.sum(output_share * output_share)
        + jnp.sum(in_share * in_share)
        + jnp.sum(gains_share * gains_share) / groups,
        ("dp", "mp"),
    )
    grad_norm = jnp.sqrt(total)
    clip = jnp.minimum(1.0, 1.0 / (grad_norm + 1e-06))
    qk_part = jnp.stack((in_share[:width].T, in_share[width : 2 * width].T)).astype(low)
    qk_share = lax.all_gather(qk_part, "mp", axis=2, tiled=True).astype(jnp.float32)
    value_share = in_share[2 * width :].T
    gate_up_share = jnp.stack((gate_share.T, up_share.T))
    root = 1.0 / math.sqrt(D)
    outs = ()
    for share, first, second, weight, average, rate in (
        (qk_share, qk_first, qk_second, qk_weight, qk_average, root),
        (value_share, value_first, value_second, value_weight, value_average, root),
        (
            output_share,
            output_first,
            output_second,
            output_weight,
            output_average,
            1.0 / math.sqrt(max(1, V_ALL * 16 // LEN)),
        ),
        (gate_up_share, gate_up_first, gate_up_second, gate_up_weight, gate_up_average, root),
        (down_share, down_first, down_second, down_weight, down_average, 1.0 / math.sqrt(FF)),
        (gains_share, gains_first, gains_second, gains, gains_average, 0.4),
    ):
        outs += adam_step(clip * share, first, second, weight, average, rate)
    return (block_out, input_grad, grad_norm) + outs


def solution(mesh):
    placed = (
        P("dp", None),
        P("dp", None),
        P(None, "dp", None),
        P(None, "dp", None),
        P(None, "dp", None),
        P(None, "dp", None),
        P("dp", "mp"),
        P("dp", "mp"),
        P("dp", "mp"),
        P("dp", "mp"),
        P("mp", "dp"),
        P("mp", "dp"),
        P("mp", "dp"),
        P("mp", "dp"),
        P(None, "dp", "mp"),
        P(None, "dp", "mp"),
        P(None, "dp", "mp"),
        P(None, "dp", "mp"),
        P("mp", "dp"),
        P("mp", "dp"),
        P("mp", "dp"),
        P("mp", "dp"),
        P(None, "dp"),
        P(None, "dp"),
        P(None, "dp"),
        P(None, "dp"),
    )
    return jax.shard_map(
        on_device,
        mesh=mesh,
        in_specs=placed,
        out_specs=(
            P("dp", "mp"),
            P("dp", "mp"),
            P(),
            P(None, "dp", None),
            P(None, "dp", None),
            P(None, "dp", None),
            P(None, "dp", None),
            P("dp", "mp"),
            P("dp", "mp"),
            P("dp", "mp"),
            P("dp", "mp"),
            P("mp", "dp"),
            P("mp", "dp"),
            P("mp", "dp"),
            P("mp", "dp"),
            P(None, "dp", "mp"),
            P(None, "dp", "mp"),
            P(None, "dp", "mp"),
            P(None, "dp", "mp"),
            P("mp", "dp"),
            P("mp", "dp"),
            P("mp", "dp"),
            P("mp", "dp"),
            P(None, "dp"),
            P(None, "dp"),
            P(None, "dp"),
            P(None, "dp"),
        ),
        check_vma=False,
    )
```

```python
import functools
import math

import jax
import jax.numpy as jnp
from jax import lax
from jax.experimental import pallas as pl
from jax.experimental.pallas import tpu as pltpu
from jax.sharding import PartitionSpec as P

D = 1024
H = 16
F = 16
VH = 64
FF = 2752
V_ALL = 1024
LEN = 1024
STEP = 5
BLOCK = 256
TOGETHER = 2


def nn(left, right):
    return lax.dot_general(
        left, right, (((1,), (0,)), ((), ())), preferred_element_type=jnp.float32
    )


def nt(left, right):
    return lax.dot_general(
        left, right, (((1,), (1,)), ((), ())), preferred_element_type=jnp.float32
    )


def tn(left, right):
    return lax.dot_general(
        left, right, (((0,), (0,)), ((), ())), preferred_element_type=jnp.float32
    )


def rms_scale(values):
    return lax.rsqrt(jnp.mean(values * values, axis=1, keepdims=True) + 1e-05)


def upper(size):
    rows = lax.broadcasted_iota(jnp.int32, (size, size), 0)
    return rows <= lax.broadcasted_iota(jnp.int32, (size, size), 1)


def spans(block):
    start = block * BLOCK
    whole = [(0, start, False)] if block else []
    return whole + [(start, start + BLOCK, True)]


def mix_forward(heads):
    keys = [head[1][...].T for head in heads]
    seen = upper(BLOCK)
    for block in range(heads[0][0].shape[1] // BLOCK):
        at = slice(block * BLOCK, (block + 1) * BLOCK)
        query = [head[0][:, at] * jnp.bfloat16(1.0 / math.sqrt(F)) for head in heads]
        numer, denom = [0.0] * len(heads), [0.0] * len(heads)
        for low, high, edge in spans(block):
            slopes = [nn(k[low:high], q) + 1.0 for k, q in zip(keys, query)]
            for i, (head, slope) in enumerate(zip(heads, slopes)):
                kernel = slope * slope + 1.0
                if edge:
                    kernel = jnp.where(seen, kernel, 0.0)
                denom[i] += jnp.sum(kernel, axis=0, keepdims=True)
                numer[i] += nn(head[2][:, low:high], kernel.astype(jnp.bfloat16))
        for i, head in enumerate(heads):
            head[3][:, at] = (numer[i] / denom[i]).astype(jnp.bfloat16)
            head[4][0, :, at] = denom[i]


def mix_backward(heads, keys_sum, values_sum):
    wide, low_type = jnp.float32, jnp.bfloat16
    root = 1.0 / math.sqrt(F)
    keys = [head[1][...].T for head in heads]
    values = [head[2][...].T for head in heads]
    seen = upper(BLOCK)
    keys_sum[...] = jnp.zeros_like(keys_sum)
    values_sum[...] = jnp.zeros_like(values_sum)
    for block in range(heads[0][0].shape[1] // BLOCK):
        at = slice(block * BLOCK, (block + 1) * BLOCK)
        query = [head[0][:, at] * low_type(root) for head in heads]
        grad_numer, grad_denom = [], []
        for head in heads:
            share = 2.0 / head[4][0, :, at]
            grad = head[5][:, at].astype(wide)
            grad_numer.append((grad * share).astype(low_type))
            total = jnp.sum(grad * head[3][:, at].astype(wide), axis=0, keepdims=True)
            grad_denom.append(-share * total)
        grad_query = [0.0] * len(heads)
        for low, high, edge in spans(block):
            slopes = [nn(k[low:high], q) + 1.0 for k, q in zip(keys, query)]
            terms = [nn(v[low:high], g) + d for v, g, d in zip(values, grad_numer, grad_denom)]
            kernels = [slope * slope + 1.0 for slope in slopes]
            tilts = [term * slope for term, slope in zip(terms, slopes)]
            if edge:
                kernels = [jnp.where(seen, kernel, 0.0) for kernel in kernels]
                tilts = [jnp.where(seen, tilt, 0.0) for tilt in tilts]
            kernels = [kernel.astype(low_type) for kernel in kernels]
            tilts = [tilt.astype(low_type) for tilt in tilts]
            for i, head in enumerate(heads):
                values_sum[i, :, low:high] += nt(grad_numer[i], kernels[i])
                keys_sum[i, :, low:high] += nt(query[i], tilts[i])
                grad_query[i] += nn(head[1][:, low:high], tilts[i])
        for i, head in enumerate(heads):
            head[6][:, at] = (grad_query[i] * root).astype(low_type)
    for i, head in enumerate(heads):
        head[7][...] = keys_sum[i].astype(low_type)
        head[8][...] = (values_sum[i] * 0.5).astype(low_type)


def attend_back_kernel(*refs):
    mix_backward([refs[:9]], *refs[9:])


def head_specs(groups, count):
    here = H // groups
    small = here * (2 * F + VH) // F
    large = here * (2 * F + VH) // VH
    skip = 2 * here * F // VH
    query = pl.BlockSpec((F, count), lambda h: (h // here * small + h % here, 0))
    keys = pl.BlockSpec((F, count), lambda h: (h // here * small + here + h % here, 0))
    values = pl.BlockSpec((VH, count), lambda h: (h // here * large + skip + h % here, 0))
    return [query, keys, values]


class Place:
    def __init__(self, side=None):
        dp, mp = lax.axis_index("dp"), lax.axis_index("mp")
        self.dp, self.mp = dp, mp
        self.z, self.x = lax.div(dp, 2), lax.rem(dp, 2)
        self.y, self.c = lax.div(mp, 2), lax.rem(mp, 2)
        self.side = self.c if side is None else side

    def at(self, turn, second, third, core=0):
        across_x = self.side * second + (1 - self.side) * third
        across_y = (1 - self.side) * second + self.side * third
        z = lax.rem(self.z + turn, 4)
        x = self.x + across_x * (1 - 2 * self.x)
        y = self.y + across_y * (1 - 2 * self.y)
        c = self.c + core * (1 - 2 * self.c)
        return (z * 2 + x, y * 2 + c)

    def diagonal(self):
        return (self.dp, 3 - self.mp)

    def across(self, turn):
        return (self.dp, lax.rem(self.mp + turn, 4))

    def greet(self, wide=False):
        barrier = pltpu.get_barrier_semaphore()
        around = [self.at(turn, 0, 0) for turn in (1, 2, 3)]
        around += [self.at(0, 1, 0), self.at(0, 0, 1), self.at(0, 0, 0, 1)]
        around += [self.diagonal()] if wide else []
        for device in around:
            pl.semaphore_signal(
                barrier, inc=1, device_id=device, device_id_type=pl.DeviceIdType.MESH
            )
        pl.semaphore_wait(barrier, len(around))


def block_of(ref, owner):
    rows, lanes = ref.shape[0] // 4, ref.shape[1] // 8
    return ref.at[
        pl.ds(pl.multiple_of(owner[1] * rows, 16), rows),
        pl.ds(pl.multiple_of(owner[0] * lanes, 128), lanes),
    ]


STEPS = (
    [(0, 0, 0)]
    + [(turn, 0, 0) for turn in (1, 2, 3)]
    + [(turn, 1, 0) for turn in range(4)]
    + [(turn, second, 1) for second in range(2) for turn in range(4)]
)


class Spread:
    def __init__(self, place, shard, full, send, recv, own):
        self.place, self.shard, self.full = place, shard, full
        self.send, self.recv, self.own = send, recv, own

    def copy(self, owner, slot, device, source=None):
        target = block_of(self.full, owner)
        return pltpu.make_async_remote_copy(
            src_ref=target if source is None else source,
            dst_ref=target,
            send_sem=self.send.at[slot],
            recv_sem=self.recv.at[owner[0] * 4 + owner[1]],
            device_id=device,
            device_id_type=pl.DeviceIdType.MESH,
        )

    def targets(self, step):
        second, third, core = (0, 1, 0), (0, 0, 1), (0, 0, 0)
        if step == 0:
            return [(turn, 0, 0, 0) for turn in (1, 2, 3)] + [
                (0, 1, 0, 0),
                (0, 0, 1, 0),
                (0, 0, 0, 1),
            ]
        if step < 4:
            return [(0, 1, 0, 0), (0, 0, 1, 0), (0, 0, 0, 1)]
        if step < 8:
            return [(0, 0, 1, 0), (0, 0, 0, 1)]
        return [(0, 0, 0, 1)]

    def slot(self, step):
        return sum(len(self.targets(earlier)) for earlier in range(step))

    def run(self, step):
        owner = self.place.at(*STEPS[step])
        slot = self.slot(step)
        if step:
            self.copy(owner, slot, owner).wait_recv()
        else:
            pltpu.make_async_copy(self.shard, block_of(self.full, owner), self.own).start()
        for more, target in enumerate(self.targets(step)):
            self.copy(
                owner, slot + more, self.place.at(*target), None if step else self.shard
            ).start()

    def finish(self):
        mine = self.place.at(0, 0, 0)
        pltpu.make_async_copy(self.shard, block_of(self.full, mine), self.own).wait()
        for turn, second, third in STEPS:
            owner = self.place.at(turn, second, third, 1)
            self.copy(owner, 0, owner).wait_recv()

    def close(self):
        mine = self.place.at(0, 0, 0)
        for slot in range(self.slot(16)):
            self.copy(mine, slot, self.place.at(0, 0, 0, 1)).wait_send()


def head_rows(head, here):
    group, place = lax.div(head, here), lax.rem(head, here)
    start = group * here * (2 * F + VH)
    query = pl.multiple_of(start + place * F, F)
    keys = pl.multiple_of(start + (here + place) * F, F)
    values = pl.multiple_of(start + 2 * here * F + place * VH, VH)
    return pl.ds(query, F), pl.ds(keys, F), pl.ds(values, VH)


def first_half(
    direct,
    groups,
    tokens,
    out_grad,
    *refs,
):
    refs = list(refs)

    def take(count):
        head, refs[:] = refs[:count], refs[count:]
        return head

    low, wide = jnp.bfloat16, jnp.float32
    masters = take(6) if direct else []
    shards = [] if direct else take(5)
    w_in, w_out, w_gate, w_up, w_down = take(5) if direct else shards
    projected_out, mixed_out, denom_out, one_out, two_out, resid_out, gain_out, grad_out = take(8)
    acts = take(3)
    x_v, grad_v, in_v, out_v, one_v, proj_v, mixed_v, denom_v, resid_v, two_v, gain_v = take(11)
    gate_v, slope_v, weight_v, act_v, load, store, weight_load, act_store = take(8)
    count = x_v.shape[0]
    hidden = w_down.shape[0] // groups
    rank = lax.axis_index("mp")
    here = H // groups
    mine = pl.ds(pl.multiple_of(rank * count, LEN), count)
    get_x = pltpu.make_async_copy(tokens.at[mine], x_v, load.at[0])
    get_grad = pltpu.make_async_copy(out_grad.at[mine], grad_v, load.at[1])
    get_x.start()
    get_grad.start()
    stores = []

    def put(source, target):
        copy = pltpu.make_async_copy(source, target, store.at[len(stores)])
        copy.start()
        stores.append(copy)

    spreads = []
    if direct:
        shards = take(5)
        turned, send, recv, own = take(4)
        place = Place()
        fulls = (in_v, out_v, w_gate, w_up, w_down)
        qk, value, output, gate_up, down, gains = masters
        width = here * F

        def prepare(i):
            if i == 0:
                part = pl.ds(pl.multiple_of(rank * width, width), width)
                for which in range(2):
                    turned[...] = qk[which].T
                    shards[0][which * width : (which + 1) * width, :] = turned[part, :].astype(low)
                values = value.shape[1]
                shards[0][2 * width : 2 * width + values, :] = value[...].T.astype(low)
                zeros = jnp.zeros((14, gains.shape[1]), wide)
                shards[0][2 * width + values : 2 * width + values + 16, :] = jnp.concatenate(
                    (gains[...], zeros), axis=0
                ).astype(low)
            elif i == 1:
                shards[1][...] = output[...].astype(low)
            elif i == 4:
                shards[4][...] = down[...].astype(low)
            else:
                shards[i][...] = gate_up[i - 2].astype(low)

        prepare(0)
        place.greet()
        spreads = [
            Spread(place, shard, full, send.at[i], recv.at[i], own.at[i])
            for i, (shard, full) in enumerate(zip(shards, fulls))
        ]

    def steps(i, first, last):
        if direct:
            for step in range(first, last):
                spreads[i].run(step)

    def arrive(i):
        if direct:
            spreads[i].finish()

    steps(0, 0, 1)
    if direct:
        prepare(1)
    steps(1, 0, 1)
    if direct:
        prepare(2)
    steps(0, 1, 4)
    steps(2, 0, 1)
    if direct:
        prepare(3)
        prepare(4)
    steps(0, 4, 8)
    steps(1, 1, 4)
    steps(0, 8, 16)
    if not direct:
        get_in = pltpu.make_async_copy(w_in, in_v, load.at[2])
        get_out = pltpu.make_async_copy(w_out, out_v, load.at[3])
        get_in.start()
        get_out.start()
    get_x.wait()
    get_grad.wait()
    put(grad_v, grad_out)
    arrive(0)
    if direct:
        put(in_v, w_in)
    else:
        get_in.wait()
        get_out.wait()
    rows_in = in_v.shape[0] // groups
    used = here * (2 * F + VH)
    gain_v[...] = in_v[used : used + 16, :].astype(wide)
    put(gain_v, gain_out)
    piece = 128

    @pl.loop(0, count // piece)
    def _(i):
        at = pl.ds(pl.multiple_of(i * piece, piece), piece)
        x = x_v[at, :].astype(wide)
        one_v[at, :] = (x * rms_scale(x) * gain_v[0:1, :]).astype(low)

    @pl.loop(0, groups)
    def _(group):
        weight = in_v[pl.ds(pl.multiple_of(group * rows_in, 16), used), :]
        proj_v[pl.ds(pl.multiple_of(group * used, 128), used), :] = nt(weight, one_v[...]).astype(
            low
        )

    put(one_v, one_out)
    put(proj_v, projected_out)
    steps(3, 0, 1)
    plan = {
        0: [(1, 4, 8)],
        1: [(2, 1, 4)],
        2: [(1, 8, 16), (4, 0, 1)],
        4: [(2, 4, 6)],
        5: [(2, 6, 8)],
        6: [(3, 1, 4)],
    }

    @pl.loop(0, H // TOGETHER)
    def _(turn):
        heads = []
        for more in range(TOGETHER):
            head = turn * TOGETHER + more
            query, keys, values = head_rows(head, here)
            mixed = mixed_v.at[pl.ds(pl.multiple_of(head * VH, VH), VH)]
            denom = denom_v.at[pl.ds(head, 1)]
            heads.append((proj_v.at[query], proj_v.at[keys], proj_v.at[values], mixed, denom))
        mix_forward(heads)
        if direct:
            for spot, items in plan.items():

                @pl.when(turn == spot)
                def _():
                    for item in items:
                        steps(*item)

    put(mixed_v, mixed_out)
    put(denom_v, denom_out)
    arrive(1)
    if direct:
        put(out_v, w_out)

    @pl.loop(0, count // 256)
    def _(i):
        at = pl.ds(pl.multiple_of(i * 256, 256), 256)
        attended = tn(mixed_v[:, at], out_v[...])
        resid = x_v[at, :].astype(wide) + attended
        resid_v[at, :] = resid
        two_v[at, :] = (resid * rms_scale(resid) * gain_v[1:2, :]).astype(low)

    put(resid_v, resid_out)
    put(two_v, two_out)

    def weight_copy(source, group, slot):
        rows = pl.ds(group * hidden, hidden)
        return pltpu.make_async_copy(source.at[rows], weight_v.at[slot], weight_load.at[slot])

    def act_copy(which, group, slot):
        rows = pl.ds(group * hidden, hidden)
        return pltpu.make_async_copy(act_v.at[slot], acts[which].at[rows], act_store.at[slot])

    def tiles(source, body):
        weight_copy(source, 0, 0).start()
        for group in range(groups):
            weight_copy(source, group, group % 2).wait()
            if group + 1 < groups:
                weight_copy(source, group + 1, (group + 1) % 2).start()
            body(group, weight_v.at[group % 2])

    def columns(body):
        @pl.loop(0, count // 256)
        def _(i):
            body(pl.ds(pl.multiple_of(i * 256, 256), 256))

    steps(2, 8, 16)
    arrive(2)

    def gate_tile(group, weight):
        rows = pl.ds(group * hidden, hidden)

        def part(at):
            gate_v[rows, at] = nt(weight[...], two_v[at, :])

        columns(part)
        steps(3, 4 + group, 5 + group)

    tiles(w_gate, gate_tile)
    steps(4, 1, 4)
    steps(3, 8, 16)
    arrive(3)

    def up_tile(group, weight):
        rows = pl.ds(group * hidden, hidden)
        slot = group % 2
        if group >= 2:
            act_copy(0, group - 2, slot).wait()

        def part(at):
            lift = nt(weight[...], two_v[at, :])
            gate = gate_v[rows, at]
            sigma = jax.nn.sigmoid(gate)
            silu = gate * sigma
            act_v[slot, :, at] = (silu * lift).astype(low)
            gate_v[rows, at] = silu
            slope_v[rows, at] = lift * sigma * (1.0 + gate * (1.0 - sigma))

        columns(part)
        act_copy(0, group, slot).start()
        steps(4, 4 + group, 5 + group)

    tiles(w_up, up_tile)
    for group in (2, 3):
        act_copy(0, group, group % 2).wait()
    steps(4, 8, 16)
    arrive(4)

    def down_tile(group, weight):
        rows = pl.ds(group * hidden, hidden)
        if group:
            act_copy(1, group - 1, 0).wait()
            act_copy(2, group - 1, 1).wait()

        def part(at):
            grad = nt(weight[...], grad_v[at, :])
            act_v[0, :, at] = (grad * slope_v[rows, at]).astype(low)
            act_v[1, :, at] = (grad * gate_v[rows, at]).astype(low)

        columns(part)
        act_copy(1, group, 0).start()
        act_copy(2, group, 1).start()

    tiles(w_down, down_tile)
    act_copy(1, groups - 1, 0).wait()
    act_copy(2, groups - 1, 1).wait()
    for spread in spreads:
        spread.close()
    for copy in stores:
        copy.wait()


def forward(tokens, out_grad, masters, shards, groups, direct):
    low, wide = jnp.bfloat16, jnp.float32
    count, depth = tokens.shape[0] // groups, tokens.shape[1]
    used = H * (2 * F + VH)
    here = H // groups
    heights = [here * (2 * F + VH) + 16, here * VH] + [masters[4].shape[0]] * 3
    fulls = [jax.ShapeDtypeStruct((rows * groups, depth), low) for rows in heights]
    outs = [
        jax.ShapeDtypeStruct((used, count), low),
        jax.ShapeDtypeStruct((H * VH, count), low),
        jax.ShapeDtypeStruct((H, 1, count), wide),
        jax.ShapeDtypeStruct((count, depth), low),
        jax.ShapeDtypeStruct((count, depth), low),
        jax.ShapeDtypeStruct((count, depth), wide),
        jax.ShapeDtypeStruct((16, depth), wide),
        jax.ShapeDtypeStruct((count, depth), low),
    ]
    hidden = fulls[4].shape[0]
    outs += [jax.ShapeDtypeStruct((hidden, count), low)] * 3
    scratch = [
        pltpu.VMEM((count, depth), low),
        pltpu.VMEM((count, depth), low),
        pltpu.VMEM(fulls[0].shape, low),
        pltpu.VMEM(fulls[1].shape, low),
        pltpu.VMEM((count, depth), low),
        pltpu.VMEM((used, count), low),
        pltpu.VMEM((H * VH, count), low),
        pltpu.VMEM((H, 1, count), wide),
        pltpu.VMEM((count, depth), wide),
        pltpu.VMEM((count, depth), low),
        pltpu.VMEM((16, depth), wide),
        pltpu.VMEM((hidden, count), wide),
        pltpu.VMEM((hidden, count), wide),
        pltpu.VMEM((2, hidden // groups, depth), low),
        pltpu.VMEM((2, hidden // groups, count), low),
        pltpu.SemaphoreType.DMA((4,)),
        pltpu.SemaphoreType.DMA((10,)),
        pltpu.SemaphoreType.DMA((2,)),
        pltpu.SemaphoreType.DMA((2,)),
    ]
    extra = {}
    if direct:
        outs = fulls + outs
        lanes = masters[4].shape[1]
        scratch += [pltpu.VMEM((rows, lanes), low) for rows in heights]
        scratch += [
            pltpu.VMEM((masters[0].shape[2], lanes), wide),
            pltpu.SemaphoreType.DMA((5, 31)),
            pltpu.SemaphoreType.DMA((5, 32)),
            pltpu.SemaphoreType.DMA((5,)),
        ]
        extra = dict(collective_id=0, has_side_effects=True)
    anywhere = pl.BlockSpec(memory_space=pl.ANY)
    results = pl.pallas_call(
        functools.partial(first_half, direct, groups),
        in_specs=[anywhere] * 2
        + ([pl.BlockSpec(memory_space=pltpu.VMEM)] * 6 if direct else [anywhere] * 5),
        out_specs=[anywhere] * len(outs),
        out_shape=outs,
        scratch_shapes=scratch,
        cost_estimate=pl.CostEstimate(
            flops=50_000_000_000, bytes_accessed=100_000_000, transcendentals=0
        ),
        compiler_params=pltpu.CompilerParams(vmem_limit_bytes=67_043_328, **extra),
        name="first_half",
    )(tokens, out_grad, *(masters if direct else shards))
    return (results[:5] if direct else list(shards)), (results[5:] if direct else results)


def attend_back(projected, mixed, denom, grad, groups):
    count = projected.shape[1]
    head = pl.BlockSpec((VH, count), lambda h: (h, 0))
    return pl.pallas_call(
        attend_back_kernel,
        grid=(H,),
        in_specs=head_specs(groups, count)
        + [head, pl.BlockSpec((1, 1, count), lambda h: (h, 0, 0)), head],
        out_specs=[
            pl.BlockSpec((F, count), lambda h: (h, 0)),
            pl.BlockSpec((F, count), lambda h: (h, 0)),
            head,
        ],
        out_shape=[
            jax.ShapeDtypeStruct((H * F, count), jnp.bfloat16),
            jax.ShapeDtypeStruct((H * F, count), jnp.bfloat16),
            jax.ShapeDtypeStruct((H * VH, count), jnp.bfloat16),
        ],
        scratch_shapes=[
            pltpu.VMEM((1, F, count), jnp.float32),
            pltpu.VMEM((1, VH, count), jnp.float32),
        ],
        cost_estimate=pl.CostEstimate(
            flops=40_000_000_000, bytes_accessed=12_000_000, transcendentals=0
        ),
        compiler_params=pltpu.CompilerParams(vmem_limit_bytes=48 << 20),
        name="attend_back",
    )(projected, projected, projected, mixed, denom, grad)


class Gathered:
    def __init__(self, place, own, given, third, second, last, send, recv):
        self.place, self.own, self.given = place, own, given
        self.third, self.second, self.last = third, second, last
        self.send, self.recv = send, recv

    def copy(self, source, target, slot, device):
        return pltpu.make_async_remote_copy(
            src_ref=source,
            dst_ref=target,
            send_sem=self.send.at[slot],
            recv_sem=self.recv.at[slot],
            device_id=device,
            device_id_type=pl.DeviceIdType.MESH,
        )

    def group(self, turn):
        core = 1 - self.place.c if turn < 2 else self.place.c
        return 2 * (turn % 2) + core

    def hand(self, tile, turn):
        return self.copy(tile, self.given.at[turn], turn, self.place.at(0, 0, 0, 1))

    def wait_given(self):
        for turn in range(2):
            self.hand(self.given.at[turn], turn).wait_recv()

    def part(self, turn, second, third):
        dp, mp = self.place.at(turn, second, third)
        side = lax.div(mp, 2)
        lanes = pl.ds(pl.multiple_of(dp * 128, 128), 128)
        return self.own.at[side, :, lanes], self.given.at[side, :, lanes]

    def run(self, step):
        wide, low = jnp.float32, jnp.bfloat16
        place = self.place
        if step < 8:
            second, turn = 1 - step // 4, step % 4
            own, given = self.part(turn, second, 1)
            own[...] = (own[...].astype(wide) + given[...].astype(wide)).astype(low)
            slot = second * 4 + turn
            self.copy(own, self.third.at[slot], 2 + slot, place.at(0, 0, 1)).start()
        elif step < 12:
            turn = step - 8
            own, given = self.part(turn, 1, 0)
            self.copy(own, self.third.at[4 + turn], 6 + turn, place.at(0, 0, 1)).wait_recv()
            own[...] = (
                own[...].astype(wide) + given[...].astype(wide) + self.third[4 + turn].astype(wide)
            ).astype(low)
            self.copy(own, self.second.at[turn], 10 + turn, place.at(0, 1, 0)).start()
        else:
            turn = (step - 11) % 4
            own, given = self.part(turn, 0, 0)
            self.copy(own, self.third.at[turn], 2 + turn, place.at(0, 0, 1)).wait_recv()
            self.copy(own, self.second.at[turn], 10 + turn, place.at(0, 1, 0)).wait_recv()
            total = (
                own[...].astype(wide)
                + given[...].astype(wide)
                + self.third[turn].astype(wide)
                + self.second[turn].astype(wide)
            )
            if turn:
                own[...] = total.astype(low)
                self.copy(own, self.last.at[turn - 1], 13 + turn, place.at(turn, 0, 0)).start()
                return None
            for other in (1, 2, 3):
                self.copy(
                    own, self.last.at[other - 1], 13 + other, place.at(other, 0, 0)
                ).wait_recv()
                total += self.last[other - 1].astype(wide)
            return total

    def close(self):
        place = self.place
        for slot in range(2, 10):
            self.copy(self.third.at[slot - 2], self.third.at[slot - 2], slot, place.at(0, 0, 1)).wait_send()
        for slot in range(10, 14):
            self.copy(
                self.second.at[slot - 10], self.second.at[slot - 10], slot, place.at(0, 1, 0)
            ).wait_send()
        for slot in range(14, 17):
            self.copy(
                self.last.at[slot - 14], self.last.at[slot - 14], slot, place.at(slot - 13, 0, 0)
            ).wait_send()


REDUCE_PLAN = {
    ("grad", 4): [(0, -1, 8)],
    ("grad", 8): [(0, 8, 10)],
    ("back", 8): [(0, 10, 12)],
    ("back", 10): [(1, -1, 8)],
    ("resid", 0): [(2, -1, 8), (0, 12, 15), (1, 8, 10)],
    ("out", 0): [(1, 10, 12)],
    ("heads", 0): [(3, -1, 8)],
    ("heads", 3): [(1, 12, 15)],
    ("heads", 4): [(2, 8, 10)],
    ("heads", 6): [(2, 10, 12)],
    ("in", 0): [(2, 12, 15), (3, 8, 12)],
    ("input", 0): [(4, -1, 8)],
    ("input", 1): [(4, 8, 10), (3, 12, 15)],
    ("input", 2): [(4, 10, 12)],
    ("input", 3): [(4, 12, 15)],
    ("end", 0): [(3, 15, 16), (2, 15, 16), (0, 15, 16), (1, 15, 16), (4, 15, 16)],
}


def second_half(groups, *refs):
    refs = list(refs)

    def take(count):
        head, refs[:] = refs[:count], refs[count:]
        return head

    low, wide = jnp.bfloat16, jnp.float32
    acts, weights = take(3), take(3)
    two, cotan, one, resid, tokens, w_in, w_out, proj, mixed, denom, gain = take(11)
    shares = take(5)
    total_out, block_out, input_out, block, grad_resid, qk_all = take(6)
    owns, givens, thirds, seconds, lasts = take(5), take(5), take(5), take(5), take(5)
    sent, act_v, pool_a, pool_b, mixed_v, pool_c, denom_v = take(7)
    keys_sum, values_sum, x_v, resid_v, meet, meet_own = take(6)
    load, act_load, send, recv, swap_send, swap_recv, meet_send, meet_recv = take(8)
    place = Place()
    count, depth = two.shape
    here = H // groups
    used = here * (2 * F + VH)
    across_x = Place(0)
    sums = [
        Gathered(across_x if i in (0, 4) else place, *parts, send.at[i], recv.at[i])
        for i, parts in enumerate(zip(owns, givens, thirds, seconds, lasts))
    ]
    place.greet(wide=True)
    loads = [0]

    def get(source, target):
        copy = pltpu.make_async_copy(source, target, load.at[loads[0]])
        loads[0] += 1
        copy.start()
        return copy

    def swap(kind, source, target, start=0):
        for turn in (1, 2, 3):
            dp, mp = place.across(turn)
            cols = pl.ds(pl.multiple_of(mp * 256, 256), 256)
            yield pltpu.make_async_remote_copy(
                src_ref=source.at[:, cols],
                dst_ref=target.at[
                    pl.ds(pl.multiple_of(place.mp * count + start, 256), source.shape[0])
                ],
                send_sem=swap_send.at[kind, turn],
                recv_sem=swap_recv.at[kind, turn],
                device_id=(dp, mp),
                device_id_type=pl.DeviceIdType.MESH,
            )

    my_cols = pl.ds(pl.multiple_of(place.mp * 256, 256), 256)
    my_rows = pl.ds(pl.multiple_of(place.mp * count, LEN), count)
    hidden = acts[0].shape[0] // groups

    def tile_copy(source, target, sem, group):
        rows = pl.ds(pl.multiple_of(group * hidden, 16), hidden)
        return pltpu.make_async_copy(source.at[rows], target, sem)

    def act_copy(tensor, group, slot):
        return tile_copy(acts[tensor], act_v.at[slot, pl.ds(0, hidden)], act_load.at[slot], group)

    order = [(tensor, turn) for tensor in range(3) for turn in range(4)]
    act_copy(0, sums[0].group(0), 0).start()
    get_cotan = get(cotan, pool_a)
    get_two = get(two, pool_b)
    waits = [get(mixed, mixed_v), get(w_out, pool_c), get(denom, denom_v)]

    def product(left, right, target):
        @pl.loop(0, 4)
        def _(i):
            at = pl.ds(pl.multiple_of(i * 256, 256), 256)
            target[:, at] = nn(left[...], right[:, at]).astype(low)

    def make(i, turn, left, right):
        rows = owns[i].shape[1]
        if turn < 2:
            tile = sent.at[turn, pl.ds(0, rows)]
            if i:
                before = owns[i - 1].shape[1]
                sums[i - 1].hand(sent.at[turn, pl.ds(0, before)], turn).wait_send()
        else:
            tile = owns[i].at[turn - 2]
        product(left, right, tile.at[pl.ds(0, left.shape[0])])
        return tile

    def steps(i, first, last):
        for step in range(first, last):
            if step == 15:
                shares[i][...] = sums[i].run(15)
            elif step == -1:
                sums[i].wait_given()
            else:
                sums[i].run(step)

    def pause(where, spot):
        for item in REDUCE_PLAN.get((where, spot), ()):
            steps(*item)

    piece = 256
    pieces = count // piece

    def hidden_back(total, weight_v, weight_load):
        def weight_copy(tensor, group, slot):
            return tile_copy(weights[tensor], weight_v.at[slot], weight_load.at[slot], group)

        def resid_copy(i, slot):
            return pltpu.make_async_copy(
                resid.at[pl.ds(i * piece, piece)], resid_v.at[slot], weight_load.at[2 + slot]
            )

        weight_copy(0, sums[0].group(0), 0).start()
        for spot, (tensor, turn) in enumerate(order):
            slot = spot % 2
            act_copy(tensor, sums[0].group(turn), slot).wait()
            weight_copy(tensor, sums[0].group(turn), slot).wait()
            if spot + 1 < len(order):
                following = order[spot + 1]
                act_copy(following[0], sums[0].group(following[1]), 1 - slot).start()
                weight_copy(following[0], sums[0].group(following[1]), 1 - slot).start()
            if spot == 0:
                get_cotan.wait()
            if spot == 4:
                get_two.wait()
            left = act_v.at[slot, pl.ds(0, hidden)]
            tile = make(tensor, turn, left, pool_b if tensor else pool_a)
            if turn < 2:
                sums[tensor].hand(tile, turn).start()
            pause("grad", spot)
            if spot in (2, 10):
                resid_copy(0, 0).start()
            fresh = spot in (0, 4)

            @pl.loop(0, pieces)
            def _(i):
                at = pl.ds(pl.multiple_of(i * piece, piece), piece)
                term = tn(act_v[slot, pl.ds(0, hidden), at], weight_v[slot])
                total[at, :] = term if fresh else total[at, :] + term

            if spot == 3:
                for i in range(pieces):
                    at = pl.ds(i * piece, piece)
                    resid_copy(i, i % 2).wait()
                    if i + 1 < pieces:
                        resid_copy(i + 1, (i + 1) % 2).start()
                    mixed_v_rows = (resid_v[i % 2] + total[at, :]).astype(low)
                    x_v[...] = mixed_v_rows
                    store = get(x_v, block.at[at])
                    local = get(
                        x_v.at[:, my_cols],
                        block_out.at[
                            pl.ds(pl.multiple_of(place.mp * count + i * piece, piece), piece)
                        ],
                    )
                    store.wait()
                    local.wait()
                for copy in swap(0, block, block_out):
                    copy.start()
            pause("back", spot)
        gain_two = jnp.zeros((1, depth), wide)
        stores = []
        for i in range(pieces):
            at = pl.ds(i * piece, piece)
            resid_copy(i, i % 2).wait()
            if i + 1 < pieces:
                resid_copy(i + 1, (i + 1) % 2).start()
            x = resid_v[i % 2]
            back = total[at, :]
            scale = rms_scale(x)
            gain_two += jnp.sum(back * (x * scale), axis=0, keepdims=True)
            back = back * gain[1:2, :]
            mean = jnp.mean(x * back, axis=1, keepdims=True)
            grad = pool_a[at, :].astype(wide) + scale * back - x * (scale * scale * scale * mean)
            total[at, :] = grad
            pool_b[at, :] = grad.astype(low)
            stores.append(get(total.at[at], grad_resid.at[at]))
        for copy in stores:
            copy.wait()
        keys_sum[0, 0:1, :] = gain_two
        pause("resid", 0)

    pl.run_scoped(
        hidden_back,
        pltpu.VMEM((count, depth), wide),
        pltpu.VMEM((2, hidden, depth), low),
        pltpu.SemaphoreType.DMA((4,)),
    )
    gain_two = keys_sum[0, 0:1, :]

    def heads_back(proj_v, back_v, grad_v):
        get_proj = get(proj, proj_v)
        get_one = get(one, pool_a)
        get_in = [
            get(
                w_in.at[pl.ds(group * (w_in.shape[0] // groups), used)],
                act_v.at[group // 2, pl.ds(group % 2 * used, used)],
            )
            for group in range(groups)
        ]
        for copy in waits:
            copy.wait()
        rows = owns[3].shape[1]
        for turn in range(4):
            left = mixed_v.at[pl.ds(pl.multiple_of(sums[3].group(turn) * rows, 128), rows)]
            tile = make(3, turn, left, pool_b)
            if turn < 2:
                sums[3].hand(tile, turn).start()

        @pl.loop(0, 4)
        def _(i):
            at = pl.ds(pl.multiple_of(i * 256, 256), 256)
            grad_v[at, :] = nt(pool_c[at, :], pool_b[...]).astype(low)

        get_proj.wait()
        pause("out", 0)

        @pl.loop(0, H // TOGETHER)
        def _(turn):
            heads = []
            for more in range(TOGETHER):
                head = turn * TOGETHER + more
                rows = head_rows(head, here)
                at = pl.ds(pl.multiple_of(head * VH, VH), VH)
                heads.append(
                    tuple(proj_v.at[row] for row in rows)
                    + (mixed_v.at[at], denom_v.at[pl.ds(head, 1)], grad_v.at[at])
                    + tuple(back_v.at[row] for row in rows)
                )
            mix_backward(heads, keys_sum, values_sum)
            for spot in range(H // TOGETHER):
                if ("heads", spot) in REDUCE_PLAN:

                    @pl.when(turn == spot)
                    def _():
                        pause("heads", spot)

        for copy in get_in:
            copy.wait()
        get_one.wait()

        def x_copies(i):
            start = pl.multiple_of(place.mp * count + i * piece, piece)
            return [
                get(tokens.at[pl.ds(start, piece)], x_v),
                get(grad_resid.at[pl.ds(i * piece, piece)], resid_v.at[i % 2]),
            ]

        keys_sum[0, 0:1, :] = jnp.zeros((1, depth), wide)

        def in_product(group, target):
            left = back_v.at[pl.ds(pl.multiple_of(group * used, 128), used)]
            weight = act_v.at[lax.div(group, 2), pl.ds(lax.rem(group, 2) * used, used)]

            @pl.loop(0, 4)
            def _(i):
                at = pl.ds(pl.multiple_of(i * 256, 256), 256)
                term = nn(left[...], pool_a[:, at])
                target[:, at] = term.astype(low)
                keys_sum[0, 0:1, at] += jnp.sum(term * weight[:, at].astype(wide), axis=0, keepdims=True)

        arrived = x_copies(0)
        tiles = []
        for turn in range(4):
            if turn < 2:
                sums[3].hand(sent.at[turn, pl.ds(0, owns[3].shape[1])], turn).wait_send()
                tiles.append(sent.at[turn, pl.ds(0, owns[4].shape[1])])
            else:
                tiles.append(owns[4].at[turn - 2])
            in_product(sums[4].group(turn), tiles[turn].at[pl.ds(0, used)])
        gain_one = keys_sum[0, 0:1, :] / gain[0:1, :]
        filler = jnp.zeros((14, depth), wide)
        gain_rows = jnp.concatenate((gain_one, gain_two, filler), axis=0).astype(low)
        for turn in range(4):
            tiles[turn][pl.ds(used, 16), :] = gain_rows
            if turn < 2:
                sums[4].hand(tiles[turn], turn).start()
        pause("in", 0)
        for i in range(pieces):
            at = pl.ds(i * piece, piece)
            back = tn(back_v[0 : 2 * used, at], act_v[0]) + tn(
                back_v[2 * used : 4 * used, at], act_v[1]
            )
            for copy in arrived:
                copy.wait()
            x = x_v[...].astype(wide)
            scale = rms_scale(x)
            back = back * gain[0:1, :]
            mean = jnp.mean(x * back, axis=1, keepdims=True)
            pool_c[at, :] = (
                resid_v[i % 2] + scale * back - x * (scale * scale * scale * mean)
            ).astype(low)
            if i + 1 < pieces:
                arrived = x_copies(i + 1)
            for copy in swap(1 + i, pool_c.at[at], input_out, i * piece):
                copy.start()
            pause("input", i)

    pl.run_scoped(
        heads_back,
        pltpu.VMEM((used * groups, count), low),
        pltpu.VMEM((used * groups, count), low),
        pltpu.VMEM((H * VH, count), low),
    )
    put_input = get(pool_c.at[:, my_cols], input_out.at[my_rows])
    pause("end", 0)
    width = here * F
    qk_copies, qk_local = [], []
    for which in range(2):
        source = shares[4].at[pl.ds(which * width, width)]
        target = qk_all.at[which, pl.ds(pl.multiple_of(place.mp * width, width), width)]
        qk_local.append(get(source, target))
        for turn in (1, 2, 3):
            qk_copies.append(
                pltpu.make_async_remote_copy(
                    src_ref=source,
                    dst_ref=target,
                    send_sem=swap_send.at[5 + which, turn],
                    recv_sem=swap_recv.at[5 + which, turn],
                    device_id=place.across(turn),
                    device_id_type=pl.DeviceIdType.MESH,
                )
            )
            qk_copies[-1].start()

    squares = jnp.zeros((8, 128), wide)
    for i, share in enumerate(shares):
        rows = used if i == 4 else share.shape[0]
        value = share[pl.ds(0, rows), :]
        squares += jnp.sum((value * value).reshape(rows // 8, 8, 128), axis=0)
    value = shares[4][pl.ds(used, 8), :]
    squares += value * value * (1.0 / groups)
    peers = [[place.at(0, 0, 0, 1)], [place.at(0, 1, 0)], [place.at(0, 0, 1)]]
    peers += [[place.at(turn, 0, 0) for turn in (1, 2, 3)]]
    slot = 0
    for level, devices in enumerate(peers):
        meet_own[level] = squares
        copies = []
        for device in devices:
            copies.append(
                pltpu.make_async_remote_copy(
                    src_ref=meet_own.at[level],
                    dst_ref=meet.at[slot],
                    send_sem=meet_send.at[slot],
                    recv_sem=meet_recv.at[slot],
                    device_id=device,
                    device_id_type=pl.DeviceIdType.MESH,
                )
            )
            slot += 1
        for copy in copies:
            copy.start()
        for more, copy in enumerate(copies):
            copy.wait()
            squares += meet[slot - len(copies) + more]
    total_out[...] = squares
    for turn in range(2):
        sums[4].hand(sent.at[turn, pl.ds(0, owns[4].shape[1])], turn).wait_send()
    for item in sums:
        item.close()
    put_input.wait()
    for copy in qk_local + qk_copies:
        copy.wait()
    for copy in swap(0, block, block_out):
        copy.wait()
    for i in range(pieces):
        for copy in swap(1 + i, pool_c.at[pl.ds(i * piece, piece)], input_out, i * piece):
            copy.wait()


def backward(groups, acts, weights, saved, resid, tokens):
    low, wide = jnp.bfloat16, jnp.float32
    w_in, w_out, *hidden_weights = weights
    projected, mixed, denom, one, two, gains_full, cotan = saved
    count, depth = two.shape
    used = H * (2 * F + VH)
    heights = [act.shape[0] // groups for act in acts] + [H * VH // groups, w_in.shape[0] // groups]
    most = max(heights)
    vmem, anywhere = pl.BlockSpec(memory_space=pltpu.VMEM), pl.BlockSpec(memory_space=pl.ANY)
    square = pltpu.VMEM((count, depth), low)
    dma = pltpu.SemaphoreType.DMA
    scratch = []
    for slots, lanes in ((2, depth), (2, depth), (8, 128), (4, 128), (3, 128)):
        scratch += [pltpu.VMEM((slots, rows, lanes), low) for rows in heights]
    scratch += [
        pltpu.VMEM((2, most, depth), low),
        pltpu.VMEM((2, max(most, used // 2), depth), low),
        square,
        square,
        square,
        square,
        pltpu.VMEM(denom.shape, wide),
        pltpu.VMEM((TOGETHER, F, count), wide),
        pltpu.VMEM((TOGETHER, VH, count), wide),
        pltpu.VMEM((256, depth), low),
        pltpu.VMEM((2, 256, depth), wide),
        pltpu.VMEM((6, 8, 128), wide),
        pltpu.VMEM((4, 8, 128), wide),
        dma((40,)),
        dma((2,)),
        dma((5, 17)),
        dma((5, 17)),
        dma((7, 4)),
        dma((7, 4)),
        dma((6,)),
        dma((6,)),
    ]
    outs = [jax.ShapeDtypeStruct((rows, 128), wide) for rows in heights]
    outs += [
        jax.ShapeDtypeStruct((8, 128), wide),
        jax.ShapeDtypeStruct((count * groups, depth // groups), low),
        jax.ShapeDtypeStruct((count * groups, depth // groups), low),
        jax.ShapeDtypeStruct((count, depth), low),
        jax.ShapeDtypeStruct((count, depth), wide),
        jax.ShapeDtypeStruct((2, H * F, 128), wide),
    ]
    results = pl.pallas_call(
        functools.partial(second_half, groups),
        in_specs=[anywhere] * 16 + [vmem],
        out_specs=[vmem] * 6 + [anywhere] * 5,
        out_shape=outs,
        scratch_shapes=scratch,
        cost_estimate=pl.CostEstimate(
            flops=80_000_000_000, bytes_accessed=100_000_000, transcendentals=0
        ),
        compiler_params=pltpu.CompilerParams(
            vmem_limit_bytes=67_043_328, collective_id=1, has_side_effects=True
        ),
        name="second_half",
    )(
        *acts,
        *hidden_weights,
        two,
        cotan,
        one,
        resid,
        tokens,
        w_in,
        w_out,
        projected,
        mixed,
        denom,
        gains_full,
    )
    return results[:8] + results[10:]


def adam_step(grad, first, second, weight, average, rate):
    first = 0.5 * first + 0.5 * grad
    second = 0.5 * second + 0.5 * grad * grad
    correct = 1.0 - 0.5**STEP
    weight = weight - rate * (first / correct / (jnp.sqrt(second / correct) + 1e-08) + 0.1 * weight)
    average = 0.5 * average + 0.5 * weight
    return (first, second, weight, average)


def update_kernel(rates, *refs):
    refs = list(refs)

    def take(count):
        head, refs[:] = refs[:count], refs[count:]
        return head

    wide = jnp.float32
    squares, qk, share_in, share_out, gate, up, down = take(7)
    block, grad = take(2)
    states = [take(4) for _ in range(6)]
    norm_out, block_out, grad_out = take(3)
    news = [take(4) for _ in range(6)]
    held = [take(4) for _ in range(6)]
    block_v, grad_v, wide_v, load, store, more = take(6)
    loads = []
    for i, (arrays, places) in enumerate(zip(states, held)):
        copies = [
            pltpu.make_async_copy(array, place, load.at[i, k])
            for k, (array, place) in enumerate(zip(arrays, places))
        ]
        for copy in copies:
            copy.start()
        loads.append(copies)
    get_block = pltpu.make_async_copy(block, block_v, more.at[0])
    get_grad = pltpu.make_async_copy(grad, grad_v, more.at[1])
    get_block.start()
    get_grad.start()
    norm = jnp.sqrt(jnp.sum(squares[...], keepdims=True))
    norm_out[...] = norm
    clip = jnp.minimum(1.0, 1.0 / (norm + 1e-06))
    width = H * F
    part = qk.shape[1] // 4
    values = share_in.shape[0] - 16 - 2 * part
    last = share_in.shape[0] - 16
    stores = []

    def update(i, share, at=slice(None)):
        first, second, weight, average = [place.at[at] for place in held[i]]
        result = adam_step(share * clip, first[...], second[...], weight[...], average[...], rates[i])
        for place, value in zip((first, second, weight, average), result):
            place[...] = value

    def finish(i):
        for k, (place, new) in enumerate(zip(held[i], news[i])):
            copy = pltpu.make_async_copy(place, new, store.at[i, k])
            copy.start()
            stores.append(copy)

    for i, parts in enumerate(
        (
            ((0, lambda: qk[0].T), (1, lambda: qk[1].T)),
            ((slice(None), lambda: share_in[pl.ds(2 * part, values), :].T),),
            ((slice(None), lambda: share_out[...]),),
            ((0, lambda: gate[...]), (1, lambda: up[...])),
            ((slice(None), lambda: down[...]),),
            ((slice(None), lambda: share_in[pl.ds(last, 8), :][:2]),),
        )
    ):
        for copy in loads[i]:
            copy.wait()
        for at, share in parts:
            update(i, share(), at)
        finish(i)
    get_block.wait()
    put_block = pltpu.make_async_copy(block_v, block_out, more.at[2])
    put_block.start()
    get_grad.wait()

    @pl.loop(0, 8)
    def _(i):
        rows = grad_v.shape[0] // 8
        at = pl.ds(pl.multiple_of(i * rows, rows), rows)
        wide_v[at, :] = grad_v[at, :].astype(wide)

    put_grad = pltpu.make_async_copy(wide_v, grad_out, more.at[3])
    put_grad.start()
    for copy in stores + [put_block, put_grad]:
        copy.wait()


def update(shares, squares, qk_all, block, grad, states, rates):
    wide = jnp.float32
    vmem, anywhere = pl.BlockSpec(memory_space=pltpu.VMEM), pl.BlockSpec(memory_space=pl.ANY)
    flat = [array for group in states for array in group]
    down, gate, up, share_out, share_in = shares
    held = [pltpu.VMEM(array.shape, wide) for array in flat]
    dma = pltpu.SemaphoreType.DMA
    norm, block, grad, *news = pl.pallas_call(
        functools.partial(update_kernel, rates),
        in_specs=[vmem] * 7 + [anywhere] * (2 + len(flat)),
        out_specs=[vmem] + [anywhere] * (2 + len(flat)),
        out_shape=[
            jax.ShapeDtypeStruct((1, 1), wide),
            jax.ShapeDtypeStruct(block.shape, block.dtype),
            jax.ShapeDtypeStruct(grad.shape, wide),
        ]
        + [jax.ShapeDtypeStruct(array.shape, wide) for array in flat],
        scratch_shapes=held
        + [
            pltpu.VMEM(block.shape, block.dtype),
            pltpu.VMEM(grad.shape, grad.dtype),
            pltpu.VMEM(grad.shape, wide),
            dma((6, 4)),
            dma((6, 4)),
            dma((4,)),
        ],
        cost_estimate=pl.CostEstimate(
            flops=20_000_000, bytes_accessed=25_000_000, transcendentals=1_000_000
        ),
        compiler_params=pltpu.CompilerParams(vmem_limit_bytes=67_043_328),
        name="update",
    )(squares, qk_all, share_in, share_out, gate, up, down, block, grad, *flat)
    return (block, grad, norm.reshape(())) + tuple(news)


def gather(shard):
    return lax.all_gather(
        lax.all_gather(shard, "dp", axis=1, tiled=True), "mp", axis=0, tiled=True
    )


def scatter(grad):
    return lax.psum_scatter(
        lax.psum_scatter(grad, "mp", scatter_dimension=0, tiled=True),
        "dp",
        scatter_dimension=1,
        tiled=True,
    )


def on_device(
    tokens,
    out_grad,
    qk_weight,
    qk_first,
    qk_second,
    qk_average,
    value_weight,
    value_first,
    value_second,
    value_average,
    output_weight,
    output_first,
    output_second,
    output_average,
    gate_up_weight,
    gate_up_first,
    gate_up_second,
    gate_up_average,
    down_weight,
    down_first,
    down_second,
    down_average,
    gains,
    gains_first,
    gains_second,
    gains_average,
):
    groups = lax.axis_size("mp")
    rank = lax.axis_index("mp")
    low = jnp.bfloat16
    here = H // groups
    count = tokens.shape[0] // groups
    assert count == LEN
    width = here * F
    masters = (
        qk_weight,
        value_weight,
        output_weight,
        jnp.swapaxes(gate_up_weight, 1, 2),
        down_weight,
        gains,
    )
    direct = (lax.axis_size("dp"), groups) == (8, 4)
    shards = ()
    if not direct:
        qk_here = lax.dynamic_slice_in_dim(qk_weight, rank * width, width, 2).astype(low)
        gain_rows = jnp.concatenate(
            (gains.astype(low), jnp.zeros((14, gains.shape[1]), low)), axis=0
        )
        shards = [
            gather(shard)
            for shard in (
                jnp.concatenate(
                    (qk_here[0].T, qk_here[1].T, value_weight.astype(low).T, gain_rows), axis=0
                ),
                output_weight.astype(low),
                gate_up_weight[0].astype(low).T,
                gate_up_weight[1].astype(low).T,
                down_weight.astype(low),
            )
        ]
    weights, saved = forward(tokens, out_grad, masters, shards, groups, direct)
    w_in, w_out, w_gate, w_up, w_down = weights
    projected, mixed, denom, hidden_one, hidden_two, resid, gains_full, cotan_low = saved[:8]
    activ, grad_gate, grad_lift = saved[8:]
    root = 1.0 / math.sqrt(D)
    rates = (root, root, 1.0 / math.sqrt(max(1, V_ALL * 16 // LEN)), root, 1.0 / math.sqrt(FF), 0.4)
    states = (
        (qk_first, qk_second, qk_weight, qk_average),
        (value_first, value_second, value_weight, value_average),
        (output_first, output_second, output_weight, output_average),
        (gate_up_first, gate_up_second, gate_up_weight, gate_up_average),
        (down_first, down_second, down_weight, down_average),
        (gains_first, gains_second, gains, gains_average),
    )
    if direct:
        *shares, squares, block_out, input_grad, qk_all = backward(
            groups,
            (activ, grad_gate, grad_lift),
            (w_in, w_out, w_down, w_gate, w_up),
            (projected, mixed, denom, hidden_one, hidden_two, gains_full, cotan_low),
            resid,
            tokens,
        )
        block_out, input_grad, grad_norm, *news = update(
            shares, squares, qk_all, block_out, input_grad, (*states[:3], tuple(jnp.swapaxes(array, 1, 2) for array in states[3]), *states[4:]), rates
        )
        news[12:16] = [jnp.swapaxes(array, 1, 2) for array in news[12:16]]
        return (block_out, input_grad, grad_norm, *news)
    first_gain, second_gain = gains_full[0], gains_full[1]
    inputs = lax.dynamic_slice_in_dim(tokens, rank * count, count, 0).astype(jnp.float32)
    scale_one = rms_scale(inputs)
    cotan = cotan_low.astype(jnp.float32)
    scale_two = rms_scale(resid)
    w_in = w_in.reshape(groups, -1, D)[:, : 6 * width].reshape(-1, D)
    block_out = (resid + tn(activ, w_down)).astype(low)
    back_two = tn(grad_gate, w_gate) + tn(grad_lift, w_up)
    gain_two = jnp.sum(back_two * resid * scale_two, axis=0)
    grad_resid = (
        cotan
        + scale_two * second_gain * back_two
        - resid * scale_two**3 * jnp.mean(resid * second_gain * back_two, axis=1, keepdims=True)
    )
    resid_low = grad_resid.astype(low)
    down_grad = nn(activ, cotan_low).astype(low)
    gate_grad = nn(grad_gate, hidden_two).astype(low)
    up_grad = nn(grad_lift, hidden_two).astype(low)
    output_grad = nn(mixed, resid_low).astype(low)
    grad_mixed = nt(w_out, resid_low).astype(low)
    grad_query, grad_keys, grad_values = attend_back(projected, mixed, denom, grad_mixed, groups)
    pieces = []
    for group in range(groups):
        pieces += [
            grad_query[group * width : (group + 1) * width],
            grad_keys[group * width : (group + 1) * width],
            grad_values[group * here * VH : (group + 1) * here * VH],
        ]
    grad_projected = jnp.concatenate(pieces, axis=0)
    in_grad = nn(grad_projected, hidden_one).astype(low)
    back_one = tn(grad_projected, w_in)
    gain_one = jnp.sum(back_one * inputs * scale_one, axis=0)
    input_grad = (
        grad_resid
        + scale_one * first_gain * back_one
        - inputs * scale_one**3 * jnp.mean(inputs * first_gain * back_one, axis=1, keepdims=True)
    ).astype(low)

    block_out = lax.all_to_all(block_out, "mp", split_axis=1, concat_axis=0, tiled=True)
    input_grad = lax.all_to_all(input_grad, "mp", split_axis=1, concat_axis=0, tiled=True).astype(
        jnp.float32
    )
    down_share = scatter(down_grad).astype(jnp.float32)
    gate_share = scatter(gate_grad).astype(jnp.float32)
    up_share = scatter(up_grad).astype(jnp.float32)
    output_share = scatter(output_grad).astype(jnp.float32)
    in_share = scatter(in_grad).astype(jnp.float32)
    gains_grad = lax.psum(jnp.stack((gain_one, gain_two)), "mp")
    gains_share = lax.psum_scatter(gains_grad, "dp", scatter_dimension=1, tiled=True)

    total = lax.psum(
        jnp.sum(down_share * down_share)
        + jnp.sum(gate_share * gate_share)
        + jnp.sum(up_share * up_share)
        + jnp.sum(output_share * output_share)
        + jnp.sum(in_share * in_share)
        + jnp.sum(gains_share * gains_share) / groups,
        ("dp", "mp"),
    )
    grad_norm = jnp.sqrt(total)
    clip = jnp.minimum(1.0, 1.0 / (grad_norm + 1e-06))
    qk_part = jnp.stack((in_share[:width].T, in_share[width : 2 * width].T)).astype(low)
    qk_share = lax.all_gather(qk_part, "mp", axis=2, tiled=True).astype(jnp.float32)
    value_share = in_share[2 * width : 6 * width].T
    gate_up_share = jnp.stack((gate_share.T, up_share.T))
    outs = ()
    gradients = (qk_share, value_share, output_share, gate_up_share, down_share, gains_share)
    for share, (first, second, weight, average), rate in zip(gradients, states, rates):
        outs += adam_step(clip * share, first, second, weight, average, rate)
    return (block_out, input_grad, grad_norm) + outs


def solution(mesh):
    placed = (
        P("dp", None),
        P("dp", None),
        P(None, "dp", None),
        P(None, "dp", None),
        P(None, "dp", None),
        P(None, "dp", None),
        P("dp", "mp"),
        P("dp", "mp"),
        P("dp", "mp"),
        P("dp", "mp"),
        P("mp", "dp"),
        P("mp", "dp"),
        P("mp", "dp"),
        P("mp", "dp"),
        P(None, "dp", "mp"),
        P(None, "dp", "mp"),
        P(None, "dp", "mp"),
        P(None, "dp", "mp"),
        P("mp", "dp"),
        P("mp", "dp"),
        P("mp", "dp"),
        P("mp", "dp"),
        P(None, "dp"),
        P(None, "dp"),
        P(None, "dp"),
        P(None, "dp"),
    )
    return jax.shard_map(
        on_device,
        mesh=mesh,
        in_specs=placed,
        out_specs=(
            P("dp", "mp"),
            P("dp", "mp"),
            P(),
            P(None, "dp", None),
            P(None, "dp", None),
            P(None, "dp", None),
            P(None, "dp", None),
            P("dp", "mp"),
            P("dp", "mp"),
            P("dp", "mp"),
            P("dp", "mp"),
            P("mp", "dp"),
            P("mp", "dp"),
            P("mp", "dp"),
            P("mp", "dp"),
            P(None, "dp", "mp"),
            P(None, "dp", "mp"),
            P(None, "dp", "mp"),
            P(None, "dp", "mp"),
            P("mp", "dp"),
            P("mp", "dp"),
            P("mp", "dp"),
            P("mp", "dp"),
            P(None, "dp"),
            P(None, "dp"),
            P(None, "dp"),
            P(None, "dp"),
        ),
        check_vma=False,
    )
```

```python
import functools
import math

import jax
import jax.numpy as jnp
from jax import lax
from jax.experimental import pallas as pl
from jax.experimental.pallas import tpu as pltpu
from jax.sharding import PartitionSpec as P

D = 1024
H = 16
F = 16
VH = 64
FF = 2752
V_ALL = 1024
LEN = 1024
STEP = 5
BLOCK = 256
TOGETHER = 2


def nn(left, right):
    return lax.dot_general(
        left, right, (((1,), (0,)), ((), ())), preferred_element_type=jnp.float32
    )


def nt(left, right):
    return lax.dot_general(
        left, right, (((1,), (1,)), ((), ())), preferred_element_type=jnp.float32
    )


def tn(left, right):
    return lax.dot_general(
        left, right, (((0,), (0,)), ((), ())), preferred_element_type=jnp.float32
    )


def rms_scale(values):
    return lax.rsqrt(jnp.mean(values * values, axis=1, keepdims=True) + 1e-05)


def upper(size):
    rows = lax.broadcasted_iota(jnp.int32, (size, size), 0)
    return rows <= lax.broadcasted_iota(jnp.int32, (size, size), 1)


def spans(block):
    start = block * BLOCK
    whole = [(0, start, False)] if block else []
    return whole + [(start, start + BLOCK, True)]


def mix_forward(heads):
    keys = [head[1][...].T for head in heads]
    seen = upper(BLOCK)
    for block in range(heads[0][0].shape[1] // BLOCK):
        at = slice(block * BLOCK, (block + 1) * BLOCK)
        query = [head[0][:, at] * jnp.bfloat16(1.0 / math.sqrt(F)) for head in heads]
        numer, denom = [0.0] * len(heads), [0.0] * len(heads)
        for low, high, edge in spans(block):
            slopes = [nn(k[low:high], q) + 1.0 for k, q in zip(keys, query)]
            for i, (head, slope) in enumerate(zip(heads, slopes)):
                kernel = slope * slope + 1.0
                if edge:
                    kernel = jnp.where(seen, kernel, 0.0)
                denom[i] += jnp.sum(kernel, axis=0, keepdims=True)
                numer[i] += nn(head[2][:, low:high], kernel.astype(jnp.bfloat16))
        for i, head in enumerate(heads):
            head[3][:, at] = (numer[i] / denom[i]).astype(jnp.bfloat16)
            head[4][0, :, at] = denom[i]


def mix_backward(heads, keys_sum, values_sum):
    wide, low_type = jnp.float32, jnp.bfloat16
    root = 1.0 / math.sqrt(F)
    keys = [head[1][...].T for head in heads]
    values = [head[2][...].T for head in heads]
    seen = upper(BLOCK)
    keys_sum[...] = jnp.zeros_like(keys_sum)
    values_sum[...] = jnp.zeros_like(values_sum)
    for block in range(heads[0][0].shape[1] // BLOCK):
        at = slice(block * BLOCK, (block + 1) * BLOCK)
        query = [head[0][:, at] * low_type(root) for head in heads]
        grad_numer, grad_denom = [], []
        for head in heads:
            share = 2.0 / head[4][0, :, at]
            grad = head[5][:, at].astype(wide)
            grad_numer.append((grad * share).astype(low_type))
            total = jnp.sum(grad * head[3][:, at].astype(wide), axis=0, keepdims=True)
            grad_denom.append(-share * total)
        grad_query = [0.0] * len(heads)
        for low, high, edge in spans(block):
            slopes = [nn(k[low:high], q) + 1.0 for k, q in zip(keys, query)]
            terms = [nn(v[low:high], g) + d for v, g, d in zip(values, grad_numer, grad_denom)]
            kernels = [slope * slope + 1.0 for slope in slopes]
            tilts = [term * slope for term, slope in zip(terms, slopes)]
            if edge:
                kernels = [jnp.where(seen, kernel, 0.0) for kernel in kernels]
                tilts = [jnp.where(seen, tilt, 0.0) for tilt in tilts]
            kernels = [kernel.astype(low_type) for kernel in kernels]
            tilts = [tilt.astype(low_type) for tilt in tilts]
            for i, head in enumerate(heads):
                values_sum[i, :, low:high] += nt(grad_numer[i], kernels[i])
                keys_sum[i, :, low:high] += nt(query[i], tilts[i])
                grad_query[i] += nn(head[1][:, low:high], tilts[i])
        for i, head in enumerate(heads):
            head[6][:, at] = (grad_query[i] * root).astype(low_type)
    for i, head in enumerate(heads):
        head[7][...] = keys_sum[i].astype(low_type)
        head[8][...] = (values_sum[i] * 0.5).astype(low_type)


def attend_back_kernel(*refs):
    mix_backward([refs[:9]], *refs[9:])


def head_specs(groups, count):
    here = H // groups
    small = here * (2 * F + VH) // F
    large = here * (2 * F + VH) // VH
    skip = 2 * here * F // VH
    query = pl.BlockSpec((F, count), lambda h: (h // here * small + h % here, 0))
    keys = pl.BlockSpec((F, count), lambda h: (h // here * small + here + h % here, 0))
    values = pl.BlockSpec((VH, count), lambda h: (h // here * large + skip + h % here, 0))
    return [query, keys, values]


class Place:
    def __init__(self, side=None):
        dp, mp = lax.axis_index("dp"), lax.axis_index("mp")
        self.dp, self.mp = dp, mp
        self.z, self.x = lax.div(dp, 2), lax.rem(dp, 2)
        self.y, self.c = lax.div(mp, 2), lax.rem(mp, 2)
        self.side = self.c if side is None else side

    def at(self, turn, second, third, core=0):
        across_x = self.side * second + (1 - self.side) * third
        across_y = (1 - self.side) * second + self.side * third
        z = lax.rem(self.z + turn, 4)
        x = self.x + across_x * (1 - 2 * self.x)
        y = self.y + across_y * (1 - 2 * self.y)
        c = self.c + core * (1 - 2 * self.c)
        return (z * 2 + x, y * 2 + c)

    def diagonal(self):
        return (self.dp, 3 - self.mp)

    def across(self, turn):
        return (self.dp, lax.rem(self.mp + turn, 4))

    def greet(self, wide=False):
        barrier = pltpu.get_barrier_semaphore()
        around = [self.at(turn, 0, 0) for turn in (1, 2, 3)]
        around += [self.at(0, 1, 0), self.at(0, 0, 1), self.at(0, 0, 0, 1)]
        around += [self.diagonal()] if wide else []
        for device in around:
            pl.semaphore_signal(
                barrier, inc=1, device_id=device, device_id_type=pl.DeviceIdType.MESH
            )
        pl.semaphore_wait(barrier, len(around))


def block_of(ref, owner):
    rows, lanes = ref.shape[0] // 4, ref.shape[1] // 8
    return ref.at[
        pl.ds(pl.multiple_of(owner[1] * rows, 16), rows),
        pl.ds(pl.multiple_of(owner[0] * lanes, 128), lanes),
    ]


STEPS = (
    [(0, 0, 0)]
    + [(turn, 0, 0) for turn in (1, 2, 3)]
    + [(turn, 1, 0) for turn in range(4)]
    + [(turn, second, 1) for second in range(2) for turn in range(4)]
)


class Spread:
    def __init__(self, place, shard, full, send, recv, own):
        self.place, self.shard, self.full = place, shard, full
        self.send, self.recv, self.own = send, recv, own

    def copy(self, owner, slot, device, source=None):
        target = block_of(self.full, owner)
        return pltpu.make_async_remote_copy(
            src_ref=target if source is None else source,
            dst_ref=target,
            send_sem=self.send.at[slot],
            recv_sem=self.recv.at[owner[0] * 4 + owner[1]],
            device_id=device,
            device_id_type=pl.DeviceIdType.MESH,
        )

    def targets(self, step):
        second, third, core = (0, 1, 0), (0, 0, 1), (0, 0, 0)
        if step == 0:
            return [(turn, 0, 0, 0) for turn in (1, 2, 3)] + [
                (0, 1, 0, 0),
                (0, 0, 1, 0),
                (0, 0, 0, 1),
            ]
        if step < 4:
            return [(0, 1, 0, 0), (0, 0, 1, 0), (0, 0, 0, 1)]
        if step < 8:
            return [(0, 0, 1, 0), (0, 0, 0, 1)]
        return [(0, 0, 0, 1)]

    def slot(self, step):
        return sum(len(self.targets(earlier)) for earlier in range(step))

    def run(self, step):
        owner = self.place.at(*STEPS[step])
        slot = self.slot(step)
        if step:
            self.copy(owner, slot, owner).wait_recv()
        else:
            pltpu.make_async_copy(self.shard, block_of(self.full, owner), self.own).start()
        for more, target in enumerate(self.targets(step)):
            self.copy(
                owner, slot + more, self.place.at(*target), None if step else self.shard
            ).start()

    def finish(self):
        mine = self.place.at(0, 0, 0)
        pltpu.make_async_copy(self.shard, block_of(self.full, mine), self.own).wait()
        for turn, second, third in STEPS:
            owner = self.place.at(turn, second, third, 1)
            self.copy(owner, 0, owner).wait_recv()

    def close(self):
        mine = self.place.at(0, 0, 0)
        for slot in range(self.slot(16)):
            self.copy(mine, slot, self.place.at(0, 0, 0, 1)).wait_send()


def head_rows(head, here):
    group, place = lax.div(head, here), lax.rem(head, here)
    start = group * here * (2 * F + VH)
    query = pl.multiple_of(start + place * F, F)
    keys = pl.multiple_of(start + (here + place) * F, F)
    values = pl.multiple_of(start + 2 * here * F + place * VH, VH)
    return pl.ds(query, F), pl.ds(keys, F), pl.ds(values, VH)


GATHER_PLAN = {
    ("start", 0): [(0, 0, 1), (2, 0, 1), (1, 0, 1), (0, 1, 12), (2, 1, 6), (3, 0, 1), (0, 12, 16)],
    ("norm", 0): [(1, 1, 4)],
    ("heads", 0): [(1, 4, 6), (4, 0, 1)],
    ("heads", 1): [(1, 6, 12)],
    ("heads", 2): [(2, 6, 8)],
    ("heads", 4): [(1, 12, 16), (3, 1, 4)],
    ("heads", 5): [(2, 8, 12)],
    ("heads", 7): [(2, 12, 16)],
    ("out", 0): [(3, 4, 6)],
    ("gate", 0): [(3, 6, 12)],
    ("gate", 2): [(4, 1, 4), (3, 12, 16)],
    ("up", 0): [(4, 4, 6)],
    ("up", 1): [(4, 6, 8)],
    ("up", 2): [(4, 8, 12)],
    ("up", 3): [(4, 12, 16)],
}


def first_half(
    direct,
    groups,
    tokens,
    out_grad,
    *refs,
):
    refs = list(refs)

    def take(count):
        head, refs[:] = refs[:count], refs[count:]
        return head

    low, wide = jnp.bfloat16, jnp.float32
    masters = take(6) if direct else []
    shards = [] if direct else take(5)
    w_in, w_out, w_gate, w_up, w_down = take(5) if direct else shards
    projected_out, mixed_out, denom_out, one_out, two_out, resid_out, gain_out, grad_out = take(8)
    acts = take(3)
    x_v, grad_v, in_v, out_v, one_v, proj_v, mixed_v, denom_v, resid_v, two_v, gain_v = take(11)
    gate_v, slope_v, weight_v, act_v, load, store, weight_load, act_store = take(8)
    count = x_v.shape[0]
    hidden = w_down.shape[0] // groups
    rank = lax.axis_index("mp")
    here = H // groups
    mine = pl.ds(pl.multiple_of(rank * count, LEN), count)
    get_x = pltpu.make_async_copy(tokens.at[mine], x_v, load.at[0])
    get_grad = pltpu.make_async_copy(out_grad.at[mine], grad_v, load.at[1])
    get_x.start()
    get_grad.start()
    stores = []

    def put(source, target):
        copy = pltpu.make_async_copy(source, target, store.at[len(stores)])
        copy.start()
        stores.append(copy)

    spreads = []
    if direct:
        shards = take(5)
        turned, send, recv, own = take(4)
        place = Place()
        fulls = (in_v, out_v, w_gate, w_up, w_down)
        qk, value, output, gate_up, down, gains = masters
        width = here * F

        def prepare(i):
            if i == 0:
                part = pl.ds(pl.multiple_of(rank * width, width), width)
                for which in range(2):
                    turned[...] = qk[which].T
                    shards[0][which * width : (which + 1) * width, :] = turned[part, :].astype(low)
                values = value.shape[1]
                shards[0][2 * width : 2 * width + values, :] = value[...].T.astype(low)
                zeros = jnp.zeros((14, gains.shape[1]), wide)
                shards[0][2 * width + values : 2 * width + values + 16, :] = jnp.concatenate(
                    (gains[...], zeros), axis=0
                ).astype(low)
            elif i == 1:
                shards[1][...] = output[...].astype(low)
            elif i == 4:
                shards[4][...] = down[...].astype(low)
            else:
                shards[i][...] = gate_up[i - 2].astype(low)

        prepare(0)
        place.greet()
        spreads = [
            Spread(place, shard, full, send.at[i], recv.at[i], own.at[i])
            for i, (shard, full) in enumerate(zip(shards, fulls))
        ]

    def arrive(i):
        if direct:
            spreads[i].finish()

    def pause(where, spot=0):
        if direct:
            for i, first, last in GATHER_PLAN.get((where, spot), ()):
                if first == 0 and i:
                    prepare(i)
                for step in range(first, last):
                    spreads[i].run(step)

    pause("start")
    if not direct:
        get_in = pltpu.make_async_copy(w_in, in_v, load.at[2])
        get_out = pltpu.make_async_copy(w_out, out_v, load.at[3])
        get_in.start()
        get_out.start()
    get_x.wait()
    get_grad.wait()
    put(grad_v, grad_out)
    arrive(0)
    if direct:
        put(in_v, w_in)
    else:
        get_in.wait()
        get_out.wait()
    rows_in = in_v.shape[0] // groups
    used = here * (2 * F + VH)
    gain_v[...] = in_v[used : used + 16, :].astype(wide)
    put(gain_v, gain_out)
    piece = 128

    @pl.loop(0, count // piece)
    def _(i):
        at = pl.ds(pl.multiple_of(i * piece, piece), piece)
        x = x_v[at, :].astype(wide)
        one_v[at, :] = (x * rms_scale(x) * gain_v[0:1, :]).astype(low)

    pause("norm")

    @pl.loop(0, groups)
    def _(group):
        weight = in_v[pl.ds(pl.multiple_of(group * rows_in, 16), used), :]
        proj_v[pl.ds(pl.multiple_of(group * used, 128), used), :] = nt(weight, one_v[...]).astype(
            low
        )

    put(one_v, one_out)
    put(proj_v, projected_out)
    pause("project")

    @pl.loop(0, H // TOGETHER)
    def _(turn):
        heads = []
        for more in range(TOGETHER):
            head = turn * TOGETHER + more
            query, keys, values = head_rows(head, here)
            mixed = mixed_v.at[pl.ds(pl.multiple_of(head * VH, VH), VH)]
            denom = denom_v.at[pl.ds(head, 1)]
            heads.append((proj_v.at[query], proj_v.at[keys], proj_v.at[values], mixed, denom))
        mix_forward(heads)
        for spot in range(H // TOGETHER):
            if direct and ("heads", spot) in GATHER_PLAN:

                @pl.when(turn == spot)
                def _():
                    pause("heads", spot)

    put(mixed_v, mixed_out)
    put(denom_v, denom_out)
    arrive(1)
    if direct:
        put(out_v, w_out)

    @pl.loop(0, count // 256)
    def _(i):
        at = pl.ds(pl.multiple_of(i * 256, 256), 256)
        attended = tn(mixed_v[:, at], out_v[...])
        resid = x_v[at, :].astype(wide) + attended
        resid_v[at, :] = resid
        two_v[at, :] = (resid * rms_scale(resid) * gain_v[1:2, :]).astype(low)

    put(resid_v, resid_out)
    put(two_v, two_out)
    pause("out")

    def weight_copy(source, group, slot):
        rows = pl.ds(group * hidden, hidden)
        return pltpu.make_async_copy(source.at[rows], weight_v.at[slot], weight_load.at[slot])

    def act_copy(which, group, slot):
        rows = pl.ds(group * hidden, hidden)
        return pltpu.make_async_copy(act_v.at[slot], acts[which].at[rows], act_store.at[slot])

    def tiles(source, body):
        weight_copy(source, 0, 0).start()
        for group in range(groups):
            weight_copy(source, group, group % 2).wait()
            if group + 1 < groups:
                weight_copy(source, group + 1, (group + 1) % 2).start()
            body(group, weight_v.at[group % 2])

    def columns(body):
        @pl.loop(0, count // 256)
        def _(i):
            body(pl.ds(pl.multiple_of(i * 256, 256), 256))

    arrive(2)

    def gate_tile(group, weight):
        rows = pl.ds(group * hidden, hidden)

        def part(at):
            gate_v[rows, at] = nt(weight[...], two_v[at, :])

        columns(part)
        pause("gate", group)

    tiles(w_gate, gate_tile)
    pause("up_start")
    arrive(3)

    def up_tile(group, weight):
        rows = pl.ds(group * hidden, hidden)
        slot = group % 2
        if group >= 2:
            act_copy(0, group - 2, slot).wait()

        def part(at):
            lift = nt(weight[...], two_v[at, :])
            gate = gate_v[rows, at]
            sigma = jax.nn.sigmoid(gate)
            silu = gate * sigma
            act_v[slot, :, at] = (silu * lift).astype(low)
            gate_v[rows, at] = silu
            slope_v[rows, at] = lift * sigma * (1.0 + gate * (1.0 - sigma))

        columns(part)
        act_copy(0, group, slot).start()
        pause("up", group)

    tiles(w_up, up_tile)
    for group in (2, 3):
        act_copy(0, group, group % 2).wait()
    pause("down_start")
    arrive(4)

    def down_tile(group, weight):
        rows = pl.ds(group * hidden, hidden)
        if group:
            act_copy(1, group - 1, 0).wait()
            act_copy(2, group - 1, 1).wait()

        def part(at):
            grad = nt(weight[...], grad_v[at, :])
            act_v[0, :, at] = (grad * slope_v[rows, at]).astype(low)
            act_v[1, :, at] = (grad * gate_v[rows, at]).astype(low)

        columns(part)
        act_copy(1, group, 0).start()
        act_copy(2, group, 1).start()

    tiles(w_down, down_tile)
    act_copy(1, groups - 1, 0).wait()
    act_copy(2, groups - 1, 1).wait()
    for spread in spreads:
        spread.close()
    for copy in stores:
        copy.wait()


def forward(tokens, out_grad, masters, shards, groups, direct):
    low, wide = jnp.bfloat16, jnp.float32
    count, depth = tokens.shape[0] // groups, tokens.shape[1]
    used = H * (2 * F + VH)
    here = H // groups
    heights = [here * (2 * F + VH) + 16, here * VH] + [masters[4].shape[0]] * 3
    fulls = [jax.ShapeDtypeStruct((rows * groups, depth), low) for rows in heights]
    outs = [
        jax.ShapeDtypeStruct((used, count), low),
        jax.ShapeDtypeStruct((H * VH, count), low),
        jax.ShapeDtypeStruct((H, 1, count), wide),
        jax.ShapeDtypeStruct((count, depth), low),
        jax.ShapeDtypeStruct((count, depth), low),
        jax.ShapeDtypeStruct((count, depth), wide),
        jax.ShapeDtypeStruct((16, depth), wide),
        jax.ShapeDtypeStruct((count, depth), low),
    ]
    hidden = fulls[4].shape[0]
    outs += [jax.ShapeDtypeStruct((hidden, count), low)] * 3
    scratch = [
        pltpu.VMEM((count, depth), low),
        pltpu.VMEM((count, depth), low),
        pltpu.VMEM(fulls[0].shape, low),
        pltpu.VMEM(fulls[1].shape, low),
        pltpu.VMEM((count, depth), low),
        pltpu.VMEM((used, count), low),
        pltpu.VMEM((H * VH, count), low),
        pltpu.VMEM((H, 1, count), wide),
        pltpu.VMEM((count, depth), wide),
        pltpu.VMEM((count, depth), low),
        pltpu.VMEM((16, depth), wide),
        pltpu.VMEM((hidden, count), wide),
        pltpu.VMEM((hidden, count), wide),
        pltpu.VMEM((2, hidden // groups, depth), low),
        pltpu.VMEM((2, hidden // groups, count), low),
        pltpu.SemaphoreType.DMA((4,)),
        pltpu.SemaphoreType.DMA((10,)),
        pltpu.SemaphoreType.DMA((2,)),
        pltpu.SemaphoreType.DMA((2,)),
    ]
    extra = {}
    if direct:
        outs = fulls + outs
        lanes = masters[4].shape[1]
        scratch += [pltpu.VMEM((rows, lanes), low) for rows in heights]
        scratch += [
            pltpu.VMEM((masters[0].shape[2], lanes), wide),
            pltpu.SemaphoreType.DMA((5, 31)),
            pltpu.SemaphoreType.DMA((5, 32)),
            pltpu.SemaphoreType.DMA((5,)),
        ]
        extra = dict(collective_id=0, has_side_effects=True)
    anywhere = pl.BlockSpec(memory_space=pl.ANY)
    results = pl.pallas_call(
        functools.partial(first_half, direct, groups),
        in_specs=[anywhere] * 2
        + ([pl.BlockSpec(memory_space=pltpu.VMEM)] * 6 if direct else [anywhere] * 5),
        out_specs=[anywhere] * len(outs),
        out_shape=outs,
        scratch_shapes=scratch,
        cost_estimate=pl.CostEstimate(
            flops=50_000_000_000, bytes_accessed=100_000_000, transcendentals=0
        ),
        compiler_params=pltpu.CompilerParams(vmem_limit_bytes=67_043_328, **extra),
        name="first_half",
    )(tokens, out_grad, *(masters if direct else shards))
    return (results[:5] if direct else list(shards)), (results[5:] if direct else results)


def attend_back(projected, mixed, denom, grad, groups):
    count = projected.shape[1]
    head = pl.BlockSpec((VH, count), lambda h: (h, 0))
    return pl.pallas_call(
        attend_back_kernel,
        grid=(H,),
        in_specs=head_specs(groups, count)
        + [head, pl.BlockSpec((1, 1, count), lambda h: (h, 0, 0)), head],
        out_specs=[
            pl.BlockSpec((F, count), lambda h: (h, 0)),
            pl.BlockSpec((F, count), lambda h: (h, 0)),
            head,
        ],
        out_shape=[
            jax.ShapeDtypeStruct((H * F, count), jnp.bfloat16),
            jax.ShapeDtypeStruct((H * F, count), jnp.bfloat16),
            jax.ShapeDtypeStruct((H * VH, count), jnp.bfloat16),
        ],
        scratch_shapes=[
            pltpu.VMEM((1, F, count), jnp.float32),
            pltpu.VMEM((1, VH, count), jnp.float32),
        ],
        cost_estimate=pl.CostEstimate(
            flops=40_000_000_000, bytes_accessed=12_000_000, transcendentals=0
        ),
        compiler_params=pltpu.CompilerParams(vmem_limit_bytes=48 << 20),
        name="attend_back",
    )(projected, projected, projected, mixed, denom, grad)


class Gathered:
    def __init__(self, place, own, given, third, second, last, send, recv):
        self.place, self.own, self.given = place, own, given
        self.third, self.second, self.last = third, second, last
        self.send, self.recv = send, recv

    def copy(self, source, target, slot, device):
        return pltpu.make_async_remote_copy(
            src_ref=source,
            dst_ref=target,
            send_sem=self.send.at[slot],
            recv_sem=self.recv.at[slot],
            device_id=device,
            device_id_type=pl.DeviceIdType.MESH,
        )

    def group(self, turn):
        core = 1 - self.place.c if turn < 2 else self.place.c
        return 2 * (turn % 2) + core

    def hand(self, tile, turn):
        return self.copy(tile, self.given.at[turn], turn, self.place.at(0, 0, 0, 1))

    def wait_given(self):
        for turn in range(2):
            self.hand(self.given.at[turn], turn).wait_recv()

    def part(self, turn, second, third):
        dp, mp = self.place.at(turn, second, third)
        side = lax.div(mp, 2)
        lanes = pl.ds(pl.multiple_of(dp * 128, 128), 128)
        return self.own.at[side, :, lanes], self.given.at[side, :, lanes]

    def run(self, step):
        wide, low = jnp.float32, jnp.bfloat16
        place = self.place
        if step < 8:
            second, turn = 1 - step // 4, step % 4
            own, given = self.part(turn, second, 1)
            own[...] = (own[...].astype(wide) + given[...].astype(wide)).astype(low)
            slot = second * 4 + turn
            self.copy(own, self.third.at[slot], 2 + slot, place.at(0, 0, 1)).start()
        elif step < 12:
            turn = step - 8
            own, given = self.part(turn, 1, 0)
            self.copy(own, self.third.at[4 + turn], 6 + turn, place.at(0, 0, 1)).wait_recv()
            own[...] = (
                own[...].astype(wide) + given[...].astype(wide) + self.third[4 + turn].astype(wide)
            ).astype(low)
            self.copy(own, self.second.at[turn], 10 + turn, place.at(0, 1, 0)).start()
        else:
            turn = (step - 11) % 4
            own, given = self.part(turn, 0, 0)
            self.copy(own, self.third.at[turn], 2 + turn, place.at(0, 0, 1)).wait_recv()
            self.copy(own, self.second.at[turn], 10 + turn, place.at(0, 1, 0)).wait_recv()
            total = (
                own[...].astype(wide)
                + given[...].astype(wide)
                + self.third[turn].astype(wide)
                + self.second[turn].astype(wide)
            )
            if turn:
                own[...] = total.astype(low)
                self.copy(own, self.last.at[turn - 1], 13 + turn, place.at(turn, 0, 0)).start()
                return None
            for other in (1, 2, 3):
                self.copy(
                    own, self.last.at[other - 1], 13 + other, place.at(other, 0, 0)
                ).wait_recv()
                total += self.last[other - 1].astype(wide)
            return total

    def close(self):
        place = self.place
        for slot in range(2, 10):
            self.copy(self.third.at[slot - 2], self.third.at[slot - 2], slot, place.at(0, 0, 1)).wait_send()
        for slot in range(10, 14):
            self.copy(
                self.second.at[slot - 10], self.second.at[slot - 10], slot, place.at(0, 1, 0)
            ).wait_send()
        for slot in range(14, 17):
            self.copy(
                self.last.at[slot - 14], self.last.at[slot - 14], slot, place.at(slot - 13, 0, 0)
            ).wait_send()


REDUCE_PLAN = {
    ("grad", 4): [(0, -1, 8)],
    ("grad", 8): [(0, 8, 10)],
    ("back", 8): [(0, 10, 12)],
    ("back", 10): [(1, -1, 8)],
    ("resid", 0): [(2, -1, 8), (0, 12, 15), (1, 8, 10)],
    ("out", 0): [(1, 10, 12)],
    ("heads", 0): [(3, -1, 8)],
    ("heads", 3): [(1, 12, 15)],
    ("heads", 4): [(2, 8, 10)],
    ("heads", 6): [(2, 10, 12)],
    ("in", 0): [(2, 12, 15), (3, 8, 12)],
    ("input", 0): [(4, -1, 8)],
    ("input", 1): [(4, 8, 10), (3, 12, 15)],
    ("input", 2): [(4, 10, 12)],
    ("input", 3): [(4, 12, 15)],
    ("end", 0): [(3, 15, 16), (2, 15, 16), (0, 15, 16), (1, 15, 16), (4, 15, 16)],
}


def second_half(groups, *refs):
    refs = list(refs)

    def take(count):
        head, refs[:] = refs[:count], refs[count:]
        return head

    low, wide = jnp.bfloat16, jnp.float32
    acts, weights = take(3), take(3)
    two, cotan, one, resid, tokens, w_in, w_out, proj, mixed, denom, gain = take(11)
    shares = take(5)
    total_out, block_out, input_out, block, grad_resid, qk_all = take(6)
    owns, givens, thirds, seconds, lasts = take(5), take(5), take(5), take(5), take(5)
    sent, act_v, pool_a, pool_b, mixed_v, pool_c, denom_v = take(7)
    keys_sum, values_sum, x_v, resid_v, meet, meet_own = take(6)
    load, act_load, send, recv, swap_send, swap_recv, meet_send, meet_recv = take(8)
    place = Place()
    count, depth = two.shape
    here = H // groups
    used = here * (2 * F + VH)
    across_x = Place(0)
    sums = [
        Gathered(across_x if i in (0, 4) else place, *parts, send.at[i], recv.at[i])
        for i, parts in enumerate(zip(owns, givens, thirds, seconds, lasts))
    ]
    place.greet(wide=True)
    loads = [0]

    def get(source, target):
        copy = pltpu.make_async_copy(source, target, load.at[loads[0]])
        loads[0] += 1
        copy.start()
        return copy

    def swap(kind, source, target, start=0):
        for turn in (1, 2, 3):
            dp, mp = place.across(turn)
            cols = pl.ds(pl.multiple_of(mp * 256, 256), 256)
            yield pltpu.make_async_remote_copy(
                src_ref=source.at[:, cols],
                dst_ref=target.at[
                    pl.ds(pl.multiple_of(place.mp * count + start, 256), source.shape[0])
                ],
                send_sem=swap_send.at[kind, turn],
                recv_sem=swap_recv.at[kind, turn],
                device_id=(dp, mp),
                device_id_type=pl.DeviceIdType.MESH,
            )

    my_cols = pl.ds(pl.multiple_of(place.mp * 256, 256), 256)
    my_rows = pl.ds(pl.multiple_of(place.mp * count, LEN), count)
    hidden = acts[0].shape[0] // groups

    def tile_copy(source, target, sem, group):
        rows = pl.ds(pl.multiple_of(group * hidden, 16), hidden)
        return pltpu.make_async_copy(source.at[rows], target, sem)

    def act_copy(tensor, group, slot):
        return tile_copy(acts[tensor], act_v.at[slot, pl.ds(0, hidden)], act_load.at[slot], group)

    order = [(tensor, turn) for tensor in range(3) for turn in range(4)]
    act_copy(0, sums[0].group(0), 0).start()
    get_cotan = get(cotan, pool_a)
    get_two = get(two, pool_b)
    waits = [get(mixed, mixed_v), get(w_out, pool_c), get(denom, denom_v)]

    def product(left, right, target):
        @pl.loop(0, 4)
        def _(i):
            at = pl.ds(pl.multiple_of(i * 256, 256), 256)
            target[:, at] = nn(left[...], right[:, at]).astype(low)

    def make(i, turn, left, right):
        rows = owns[i].shape[1]
        if turn < 2:
            tile = sent.at[turn, pl.ds(0, rows)]
            if i:
                before = owns[i - 1].shape[1]
                sums[i - 1].hand(sent.at[turn, pl.ds(0, before)], turn).wait_send()
        else:
            tile = owns[i].at[turn - 2]
        product(left, right, tile.at[pl.ds(0, left.shape[0])])
        return tile

    def steps(i, first, last):
        for step in range(first, last):
            if step == 15:
                shares[i][...] = sums[i].run(15)
            elif step == -1:
                sums[i].wait_given()
            else:
                sums[i].run(step)

    def pause(where, spot):
        for item in REDUCE_PLAN.get((where, spot), ()):
            steps(*item)

    piece = 256
    pieces = count // piece

    def hidden_back(total, weight_v, weight_load):
        def weight_copy(tensor, group, slot):
            return tile_copy(weights[tensor], weight_v.at[slot], weight_load.at[slot], group)

        def resid_copy(i, slot):
            return pltpu.make_async_copy(
                resid.at[pl.ds(i * piece, piece)], resid_v.at[slot], weight_load.at[2 + slot]
            )

        weight_copy(0, sums[0].group(0), 0).start()
        for spot, (tensor, turn) in enumerate(order):
            slot = spot % 2
            act_copy(tensor, sums[0].group(turn), slot).wait()
            weight_copy(tensor, sums[0].group(turn), slot).wait()
            if spot + 1 < len(order):
                following = order[spot + 1]
                act_copy(following[0], sums[0].group(following[1]), 1 - slot).start()
                weight_copy(following[0], sums[0].group(following[1]), 1 - slot).start()
            if spot == 0:
                get_cotan.wait()
            if spot == 4:
                get_two.wait()
            left = act_v.at[slot, pl.ds(0, hidden)]
            tile = make(tensor, turn, left, pool_b if tensor else pool_a)
            if turn < 2:
                sums[tensor].hand(tile, turn).start()
            pause("grad", spot)
            if spot in (2, 10):
                resid_copy(0, 0).start()
            fresh = spot in (0, 4)

            @pl.loop(0, pieces)
            def _(i):
                at = pl.ds(pl.multiple_of(i * piece, piece), piece)
                term = tn(act_v[slot, pl.ds(0, hidden), at], weight_v[slot])
                total[at, :] = term if fresh else total[at, :] + term

            if spot == 3:
                for i in range(pieces):
                    at = pl.ds(i * piece, piece)
                    resid_copy(i, i % 2).wait()
                    if i + 1 < pieces:
                        resid_copy(i + 1, (i + 1) % 2).start()
                    mixed_v_rows = (resid_v[i % 2] + total[at, :]).astype(low)
                    x_v[...] = mixed_v_rows
                    store = get(x_v, block.at[at])
                    local = get(
                        x_v.at[:, my_cols],
                        block_out.at[
                            pl.ds(pl.multiple_of(place.mp * count + i * piece, piece), piece)
                        ],
                    )
                    store.wait()
                    local.wait()
                for copy in swap(0, block, block_out):
                    copy.start()
            pause("back", spot)
        gain_two = jnp.zeros((1, depth), wide)
        stores = []
        for i in range(pieces):
            at = pl.ds(i * piece, piece)
            resid_copy(i, i % 2).wait()
            if i + 1 < pieces:
                resid_copy(i + 1, (i + 1) % 2).start()
            x = resid_v[i % 2]
            back = total[at, :]
            scale = rms_scale(x)
            gain_two += jnp.sum(back * (x * scale), axis=0, keepdims=True)
            back = back * gain[1:2, :]
            mean = jnp.mean(x * back, axis=1, keepdims=True)
            grad = pool_a[at, :].astype(wide) + scale * back - x * (scale * scale * scale * mean)
            total[at, :] = grad
            pool_b[at, :] = grad.astype(low)
            stores.append(get(total.at[at], grad_resid.at[at]))
        for copy in stores:
            copy.wait()
        keys_sum[0, 0:1, :] = gain_two
        pause("resid", 0)

    pl.run_scoped(
        hidden_back,
        pltpu.VMEM((count, depth), wide),
        pltpu.VMEM((2, hidden, depth), low),
        pltpu.SemaphoreType.DMA((4,)),
    )
    gain_two = keys_sum[0, 0:1, :]

    def heads_back(proj_v, back_v, grad_v):
        get_proj = get(proj, proj_v)
        get_one = get(one, pool_a)
        get_in = [
            get(
                w_in.at[pl.ds(group * (w_in.shape[0] // groups), used)],
                act_v.at[group // 2, pl.ds(group % 2 * used, used)],
            )
            for group in range(groups)
        ]
        for copy in waits:
            copy.wait()
        rows = owns[3].shape[1]
        for turn in range(4):
            left = mixed_v.at[pl.ds(pl.multiple_of(sums[3].group(turn) * rows, 128), rows)]
            tile = make(3, turn, left, pool_b)
            if turn < 2:
                sums[3].hand(tile, turn).start()

        @pl.loop(0, 4)
        def _(i):
            at = pl.ds(pl.multiple_of(i * 256, 256), 256)
            grad_v[at, :] = nt(pool_c[at, :], pool_b[...]).astype(low)

        get_proj.wait()
        pause("out", 0)

        @pl.loop(0, H // TOGETHER)
        def _(turn):
            heads = []
            for more in range(TOGETHER):
                head = turn * TOGETHER + more
                rows = head_rows(head, here)
                at = pl.ds(pl.multiple_of(head * VH, VH), VH)
                heads.append(
                    tuple(proj_v.at[row] for row in rows)
                    + (mixed_v.at[at], denom_v.at[pl.ds(head, 1)], grad_v.at[at])
                    + tuple(back_v.at[row] for row in rows)
                )
            mix_backward(heads, keys_sum, values_sum)
            for spot in range(H // TOGETHER):
                if ("heads", spot) in REDUCE_PLAN:

                    @pl.when(turn == spot)
                    def _():
                        pause("heads", spot)

        for copy in get_in:
            copy.wait()
        get_one.wait()

        def x_copies(i):
            start = pl.multiple_of(place.mp * count + i * piece, piece)
            return [
                get(tokens.at[pl.ds(start, piece)], x_v),
                get(grad_resid.at[pl.ds(i * piece, piece)], resid_v.at[i % 2]),
            ]

        keys_sum[0, 0:1, :] = jnp.zeros((1, depth), wide)

        def in_product(group, target):
            left = back_v.at[pl.ds(pl.multiple_of(group * used, 128), used)]
            weight = act_v.at[lax.div(group, 2), pl.ds(lax.rem(group, 2) * used, used)]

            @pl.loop(0, 4)
            def _(i):
                at = pl.ds(pl.multiple_of(i * 256, 256), 256)
                term = nn(left[...], pool_a[:, at])
                target[:, at] = term.astype(low)
                keys_sum[0, 0:1, at] += jnp.sum(term * weight[:, at].astype(wide), axis=0, keepdims=True)

        arrived = x_copies(0)
        tiles = []
        for turn in range(4):
            if turn < 2:
                sums[3].hand(sent.at[turn, pl.ds(0, owns[3].shape[1])], turn).wait_send()
                tiles.append(sent.at[turn, pl.ds(0, owns[4].shape[1])])
            else:
                tiles.append(owns[4].at[turn - 2])
            in_product(sums[4].group(turn), tiles[turn].at[pl.ds(0, used)])
        gain_one = keys_sum[0, 0:1, :] / gain[0:1, :]
        filler = jnp.zeros((14, depth), wide)
        gain_rows = jnp.concatenate((gain_one, gain_two, filler), axis=0).astype(low)
        for turn in range(4):
            tiles[turn][pl.ds(used, 16), :] = gain_rows
            if turn < 2:
                sums[4].hand(tiles[turn], turn).start()
        pause("in", 0)
        for i in range(pieces):
            at = pl.ds(i * piece, piece)
            back = tn(back_v[0 : 2 * used, at], act_v[0]) + tn(
                back_v[2 * used : 4 * used, at], act_v[1]
            )
            for copy in arrived:
                copy.wait()
            x = x_v[...].astype(wide)
            scale = rms_scale(x)
            back = back * gain[0:1, :]
            mean = jnp.mean(x * back, axis=1, keepdims=True)
            pool_c[at, :] = (
                resid_v[i % 2] + scale * back - x * (scale * scale * scale * mean)
            ).astype(low)
            if i + 1 < pieces:
                arrived = x_copies(i + 1)
            for copy in swap(1 + i, pool_c.at[at], input_out, i * piece):
                copy.start()
            pause("input", i)

    pl.run_scoped(
        heads_back,
        pltpu.VMEM((used * groups, count), low),
        pltpu.VMEM((used * groups, count), low),
        pltpu.VMEM((H * VH, count), low),
    )
    put_input = get(pool_c.at[:, my_cols], input_out.at[my_rows])
    pause("end", 0)
    width = here * F
    qk_copies, qk_local = [], []
    for which in range(2):
        source = shares[4].at[pl.ds(which * width, width)]
        target = qk_all.at[which, pl.ds(pl.multiple_of(place.mp * width, width), width)]
        qk_local.append(get(source, target))
        for turn in (1, 2, 3):
            qk_copies.append(
                pltpu.make_async_remote_copy(
                    src_ref=source,
                    dst_ref=target,
                    send_sem=swap_send.at[5 + which, turn],
                    recv_sem=swap_recv.at[5 + which, turn],
                    device_id=place.across(turn),
                    device_id_type=pl.DeviceIdType.MESH,
                )
            )
            qk_copies[-1].start()

    squares = jnp.zeros((8, 128), wide)
    for i, share in enumerate(shares):
        rows = used if i == 4 else share.shape[0]
        value = share[pl.ds(0, rows), :]
        squares += jnp.sum((value * value).reshape(rows // 8, 8, 128), axis=0)
    value = shares[4][pl.ds(used, 8), :]
    squares += value * value * (1.0 / groups)
    peers = [[place.at(0, 0, 0, 1)], [place.at(0, 1, 0)], [place.at(0, 0, 1)]]
    peers += [[place.at(turn, 0, 0) for turn in (1, 2, 3)]]
    slot = 0
    for level, devices in enumerate(peers):
        meet_own[level] = squares
        copies = []
        for device in devices:
            copies.append(
                pltpu.make_async_remote_copy(
                    src_ref=meet_own.at[level],
                    dst_ref=meet.at[slot],
                    send_sem=meet_send.at[slot],
                    recv_sem=meet_recv.at[slot],
                    device_id=device,
                    device_id_type=pl.DeviceIdType.MESH,
                )
            )
            slot += 1
        for copy in copies:
            copy.start()
        for more, copy in enumerate(copies):
            copy.wait()
            squares += meet[slot - len(copies) + more]
    total_out[...] = squares
    for turn in range(2):
        sums[4].hand(sent.at[turn, pl.ds(0, owns[4].shape[1])], turn).wait_send()
    for item in sums:
        item.close()
    put_input.wait()
    for copy in qk_local + qk_copies:
        copy.wait()
    for copy in swap(0, block, block_out):
        copy.wait()
    for i in range(pieces):
        for copy in swap(1 + i, pool_c.at[pl.ds(i * piece, piece)], input_out, i * piece):
            copy.wait()


def backward(groups, acts, weights, saved, resid, tokens):
    low, wide = jnp.bfloat16, jnp.float32
    w_in, w_out, *hidden_weights = weights
    projected, mixed, denom, one, two, gains_full, cotan = saved
    count, depth = two.shape
    used = H * (2 * F + VH)
    heights = [act.shape[0] // groups for act in acts] + [H * VH // groups, w_in.shape[0] // groups]
    most = max(heights)
    vmem, anywhere = pl.BlockSpec(memory_space=pltpu.VMEM), pl.BlockSpec(memory_space=pl.ANY)
    square = pltpu.VMEM((count, depth), low)
    dma = pltpu.SemaphoreType.DMA
    scratch = []
    for slots, lanes in ((2, depth), (2, depth), (8, 128), (4, 128), (3, 128)):
        scratch += [pltpu.VMEM((slots, rows, lanes), low) for rows in heights]
    scratch += [
        pltpu.VMEM((2, most, depth), low),
        pltpu.VMEM((2, max(most, used // 2), depth), low),
        square,
        square,
        square,
        square,
        pltpu.VMEM(denom.shape, wide),
        pltpu.VMEM((TOGETHER, F, count), wide),
        pltpu.VMEM((TOGETHER, VH, count), wide),
        pltpu.VMEM((256, depth), low),
        pltpu.VMEM((2, 256, depth), wide),
        pltpu.VMEM((6, 8, 128), wide),
        pltpu.VMEM((4, 8, 128), wide),
        dma((40,)),
        dma((2,)),
        dma((5, 17)),
        dma((5, 17)),
        dma((7, 4)),
        dma((7, 4)),
        dma((6,)),
        dma((6,)),
    ]
    outs = [jax.ShapeDtypeStruct((rows, 128), wide) for rows in heights]
    outs += [
        jax.ShapeDtypeStruct((8, 128), wide),
        jax.ShapeDtypeStruct((count * groups, depth // groups), low),
        jax.ShapeDtypeStruct((count * groups, depth // groups), low),
        jax.ShapeDtypeStruct((count, depth), low),
        jax.ShapeDtypeStruct((count, depth), wide),
        jax.ShapeDtypeStruct((2, H * F, 128), wide),
    ]
    results = pl.pallas_call(
        functools.partial(second_half, groups),
        in_specs=[anywhere] * 16 + [vmem],
        out_specs=[vmem] * 6 + [anywhere] * 5,
        out_shape=outs,
        scratch_shapes=scratch,
        cost_estimate=pl.CostEstimate(
            flops=80_000_000_000, bytes_accessed=100_000_000, transcendentals=0
        ),
        compiler_params=pltpu.CompilerParams(
            vmem_limit_bytes=67_043_328, collective_id=1, has_side_effects=True
        ),
        name="second_half",
    )(
        *acts,
        *hidden_weights,
        two,
        cotan,
        one,
        resid,
        tokens,
        w_in,
        w_out,
        projected,
        mixed,
        denom,
        gains_full,
    )
    return results[:8] + results[10:]


def adam_step(grad, first, second, weight, average, rate):
    first = 0.5 * first + 0.5 * grad
    second = 0.5 * second + 0.5 * grad * grad
    correct = 1.0 - 0.5**STEP
    weight = weight - rate * (first / correct / (jnp.sqrt(second / correct) + 1e-08) + 0.1 * weight)
    average = 0.5 * average + 0.5 * weight
    return (first, second, weight, average)


def update_kernel(rates, *refs):
    refs = list(refs)

    def take(count):
        head, refs[:] = refs[:count], refs[count:]
        return head

    wide = jnp.float32
    squares, qk, share_in, share_out, gate, up, down = take(7)
    block, grad = take(2)
    states = [take(4) for _ in range(6)]
    norm_out, block_out, grad_out = take(3)
    news = [take(4) for _ in range(6)]
    held = [take(4) for _ in range(6)]
    block_v, grad_v, wide_v, load, store, more = take(6)
    loads = []
    for i, (arrays, places) in enumerate(zip(states, held)):
        copies = [
            pltpu.make_async_copy(array, place, load.at[i, k])
            for k, (array, place) in enumerate(zip(arrays, places))
        ]
        for copy in copies:
            copy.start()
        loads.append(copies)
    get_block = pltpu.make_async_copy(block, block_v, more.at[0])
    get_grad = pltpu.make_async_copy(grad, grad_v, more.at[1])
    get_block.start()
    get_grad.start()
    norm = jnp.sqrt(jnp.sum(squares[...], keepdims=True))
    norm_out[...] = norm
    clip = jnp.minimum(1.0, 1.0 / (norm + 1e-06))
    width = H * F
    part = qk.shape[1] // 4
    values = share_in.shape[0] - 16 - 2 * part
    last = share_in.shape[0] - 16
    stores = []

    def update(i, share, at=slice(None)):
        first, second, weight, average = [place.at[at] for place in held[i]]
        result = adam_step(share * clip, first[...], second[...], weight[...], average[...], rates[i])
        for place, value in zip((first, second, weight, average), result):
            place[...] = value

    def finish(i):
        for k, (place, new) in enumerate(zip(held[i], news[i])):
            copy = pltpu.make_async_copy(place, new, store.at[i, k])
            copy.start()
            stores.append(copy)

    for i, parts in enumerate(
        (
            ((0, lambda: qk[0].T), (1, lambda: qk[1].T)),
            ((slice(None), lambda: share_in[pl.ds(2 * part, values), :].T),),
            ((slice(None), lambda: share_out[...]),),
            ((0, lambda: gate[...]), (1, lambda: up[...])),
            ((slice(None), lambda: down[...]),),
            ((slice(None), lambda: share_in[pl.ds(last, 8), :][:2]),),
        )
    ):
        for copy in loads[i]:
            copy.wait()
        for at, share in parts:
            update(i, share(), at)
        finish(i)
    get_block.wait()
    put_block = pltpu.make_async_copy(block_v, block_out, more.at[2])
    put_block.start()
    get_grad.wait()

    @pl.loop(0, 8)
    def _(i):
        rows = grad_v.shape[0] // 8
        at = pl.ds(pl.multiple_of(i * rows, rows), rows)
        wide_v[at, :] = grad_v[at, :].astype(wide)

    put_grad = pltpu.make_async_copy(wide_v, grad_out, more.at[3])
    put_grad.start()
    for copy in stores + [put_block, put_grad]:
        copy.wait()


def update(shares, squares, qk_all, block, grad, states, rates):
    wide = jnp.float32
    vmem, anywhere = pl.BlockSpec(memory_space=pltpu.VMEM), pl.BlockSpec(memory_space=pl.ANY)
    flat = [array for group in states for array in group]
    down, gate, up, share_out, share_in = shares
    held = [pltpu.VMEM(array.shape, wide) for array in flat]
    dma = pltpu.SemaphoreType.DMA
    norm, block, grad, *news = pl.pallas_call(
        functools.partial(update_kernel, rates),
        in_specs=[vmem] * 7 + [anywhere] * (2 + len(flat)),
        out_specs=[vmem] + [anywhere] * (2 + len(flat)),
        out_shape=[
            jax.ShapeDtypeStruct((1, 1), wide),
            jax.ShapeDtypeStruct(block.shape, block.dtype),
            jax.ShapeDtypeStruct(grad.shape, wide),
        ]
        + [jax.ShapeDtypeStruct(array.shape, wide) for array in flat],
        scratch_shapes=held
        + [
            pltpu.VMEM(block.shape, block.dtype),
            pltpu.VMEM(grad.shape, grad.dtype),
            pltpu.VMEM(grad.shape, wide),
            dma((6, 4)),
            dma((6, 4)),
            dma((4,)),
        ],
        cost_estimate=pl.CostEstimate(
            flops=20_000_000, bytes_accessed=25_000_000, transcendentals=1_000_000
        ),
        compiler_params=pltpu.CompilerParams(vmem_limit_bytes=67_043_328),
        name="update",
    )(squares, qk_all, share_in, share_out, gate, up, down, block, grad, *flat)
    return (block, grad, norm.reshape(())) + tuple(news)


def gather(shard):
    return lax.all_gather(
        lax.all_gather(shard, "dp", axis=1, tiled=True), "mp", axis=0, tiled=True
    )


def scatter(grad):
    return lax.psum_scatter(
        lax.psum_scatter(grad, "mp", scatter_dimension=0, tiled=True),
        "dp",
        scatter_dimension=1,
        tiled=True,
    )


def on_device(
    tokens,
    out_grad,
    qk_weight,
    qk_first,
    qk_second,
    qk_average,
    value_weight,
    value_first,
    value_second,
    value_average,
    output_weight,
    output_first,
    output_second,
    output_average,
    gate_up_weight,
    gate_up_first,
    gate_up_second,
    gate_up_average,
    down_weight,
    down_first,
    down_second,
    down_average,
    gains,
    gains_first,
    gains_second,
    gains_average,
):
    groups = lax.axis_size("mp")
    rank = lax.axis_index("mp")
    low = jnp.bfloat16
    here = H // groups
    count = tokens.shape[0] // groups
    assert count == LEN
    width = here * F
    masters = (
        qk_weight,
        value_weight,
        output_weight,
        jnp.swapaxes(gate_up_weight, 1, 2),
        down_weight,
        gains,
    )
    direct = (lax.axis_size("dp"), groups) == (8, 4)
    shards = ()
    if not direct:
        qk_here = lax.dynamic_slice_in_dim(qk_weight, rank * width, width, 2).astype(low)
        gain_rows = jnp.concatenate(
            (gains.astype(low), jnp.zeros((14, gains.shape[1]), low)), axis=0
        )
        shards = [
            gather(shard)
            for shard in (
                jnp.concatenate(
                    (qk_here[0].T, qk_here[1].T, value_weight.astype(low).T, gain_rows), axis=0
                ),
                output_weight.astype(low),
                gate_up_weight[0].astype(low).T,
                gate_up_weight[1].astype(low).T,
                down_weight.astype(low),
            )
        ]
    weights, saved = forward(tokens, out_grad, masters, shards, groups, direct)
    w_in, w_out, w_gate, w_up, w_down = weights
    projected, mixed, denom, hidden_one, hidden_two, resid, gains_full, cotan_low = saved[:8]
    activ, grad_gate, grad_lift = saved[8:]
    root = 1.0 / math.sqrt(D)
    rates = (root, root, 1.0 / math.sqrt(max(1, V_ALL * 16 // LEN)), root, 1.0 / math.sqrt(FF), 0.4)
    states = (
        (qk_first, qk_second, qk_weight, qk_average),
        (value_first, value_second, value_weight, value_average),
        (output_first, output_second, output_weight, output_average),
        (gate_up_first, gate_up_second, gate_up_weight, gate_up_average),
        (down_first, down_second, down_weight, down_average),
        (gains_first, gains_second, gains, gains_average),
    )
    if direct:
        *shares, squares, block_out, input_grad, qk_all = backward(
            groups,
            (activ, grad_gate, grad_lift),
            (w_in, w_out, w_down, w_gate, w_up),
            (projected, mixed, denom, hidden_one, hidden_two, gains_full, cotan_low),
            resid,
            tokens,
        )
        block_out, input_grad, grad_norm, *news = update(
            shares, squares, qk_all, block_out, input_grad, (*states[:3], tuple(jnp.swapaxes(array, 1, 2) for array in states[3]), *states[4:]), rates
        )
        news[12:16] = [jnp.swapaxes(array, 1, 2) for array in news[12:16]]
        return (block_out, input_grad, grad_norm, *news)
    first_gain, second_gain = gains_full[0], gains_full[1]
    inputs = lax.dynamic_slice_in_dim(tokens, rank * count, count, 0).astype(jnp.float32)
    scale_one = rms_scale(inputs)
    cotan = cotan_low.astype(jnp.float32)
    scale_two = rms_scale(resid)
    w_in = w_in.reshape(groups, -1, D)[:, : 6 * width].reshape(-1, D)
    block_out = (resid + tn(activ, w_down)).astype(low)
    back_two = tn(grad_gate, w_gate) + tn(grad_lift, w_up)
    gain_two = jnp.sum(back_two * resid * scale_two, axis=0)
    grad_resid = (
        cotan
        + scale_two * second_gain * back_two
        - resid * scale_two**3 * jnp.mean(resid * second_gain * back_two, axis=1, keepdims=True)
    )
    resid_low = grad_resid.astype(low)
    down_grad = nn(activ, cotan_low).astype(low)
    gate_grad = nn(grad_gate, hidden_two).astype(low)
    up_grad = nn(grad_lift, hidden_two).astype(low)
    output_grad = nn(mixed, resid_low).astype(low)
    grad_mixed = nt(w_out, resid_low).astype(low)
    grad_query, grad_keys, grad_values = attend_back(projected, mixed, denom, grad_mixed, groups)
    pieces = []
    for group in range(groups):
        pieces += [
            grad_query[group * width : (group + 1) * width],
            grad_keys[group * width : (group + 1) * width],
            grad_values[group * here * VH : (group + 1) * here * VH],
        ]
    grad_projected = jnp.concatenate(pieces, axis=0)
    in_grad = nn(grad_projected, hidden_one).astype(low)
    back_one = tn(grad_projected, w_in)
    gain_one = jnp.sum(back_one * inputs * scale_one, axis=0)
    input_grad = (
        grad_resid
        + scale_one * first_gain * back_one
        - inputs * scale_one**3 * jnp.mean(inputs * first_gain * back_one, axis=1, keepdims=True)
    ).astype(low)

    block_out = lax.all_to_all(block_out, "mp", split_axis=1, concat_axis=0, tiled=True)
    input_grad = lax.all_to_all(input_grad, "mp", split_axis=1, concat_axis=0, tiled=True).astype(
        jnp.float32
    )
    down_share = scatter(down_grad).astype(jnp.float32)
    gate_share = scatter(gate_grad).astype(jnp.float32)
    up_share = scatter(up_grad).astype(jnp.float32)
    output_share = scatter(output_grad).astype(jnp.float32)
    in_share = scatter(in_grad).astype(jnp.float32)
    gains_grad = lax.psum(jnp.stack((gain_one, gain_two)), "mp")
    gains_share = lax.psum_scatter(gains_grad, "dp", scatter_dimension=1, tiled=True)

    total = lax.psum(
        jnp.sum(down_share * down_share)
        + jnp.sum(gate_share * gate_share)
        + jnp.sum(up_share * up_share)
        + jnp.sum(output_share * output_share)
        + jnp.sum(in_share * in_share)
        + jnp.sum(gains_share * gains_share) / groups,
        ("dp", "mp"),
    )
    grad_norm = jnp.sqrt(total)
    clip = jnp.minimum(1.0, 1.0 / (grad_norm + 1e-06))
    qk_part = jnp.stack((in_share[:width].T, in_share[width : 2 * width].T)).astype(low)
    qk_share = lax.all_gather(qk_part, "mp", axis=2, tiled=True).astype(jnp.float32)
    value_share = in_share[2 * width : 6 * width].T
    gate_up_share = jnp.stack((gate_share.T, up_share.T))
    outs = ()
    gradients = (qk_share, value_share, output_share, gate_up_share, down_share, gains_share)
    for share, (first, second, weight, average), rate in zip(gradients, states, rates):
        outs += adam_step(clip * share, first, second, weight, average, rate)
    return (block_out, input_grad, grad_norm) + outs


def solution(mesh):
    placed = (
        P("dp", None),
        P("dp", None),
        P(None, "dp", None),
        P(None, "dp", None),
        P(None, "dp", None),
        P(None, "dp", None),
        P("dp", "mp"),
        P("dp", "mp"),
        P("dp", "mp"),
        P("dp", "mp"),
        P("mp", "dp"),
        P("mp", "dp"),
        P("mp", "dp"),
        P("mp", "dp"),
        P(None, "dp", "mp"),
        P(None, "dp", "mp"),
        P(None, "dp", "mp"),
        P(None, "dp", "mp"),
        P("mp", "dp"),
        P("mp", "dp"),
        P("mp", "dp"),
        P("mp", "dp"),
        P(None, "dp"),
        P(None, "dp"),
        P(None, "dp"),
        P(None, "dp"),
    )
    return jax.shard_map(
        on_device,
        mesh=mesh,
        in_specs=placed,
        out_specs=(
            P("dp", "mp"),
            P("dp", "mp"),
            P(),
            P(None, "dp", None),
            P(None, "dp", None),
            P(None, "dp", None),
            P(None, "dp", None),
            P("dp", "mp"),
            P("dp", "mp"),
            P("dp", "mp"),
            P("dp", "mp"),
            P("mp", "dp"),
            P("mp", "dp"),
            P("mp", "dp"),
            P("mp", "dp"),
            P(None, "dp", "mp"),
            P(None, "dp", "mp"),
            P(None, "dp", "mp"),
            P(None, "dp", "mp"),
            P("mp", "dp"),
            P("mp", "dp"),
            P("mp", "dp"),
            P("mp", "dp"),
            P(None, "dp"),
            P(None, "dp"),
            P(None, "dp"),
            P(None, "dp"),
        ),
        check_vma=False,
    )
```
